256 devices in a mesh: dp: 4 (over z_lo), ctx: 64 (over z_hi, x, y, core).
Axes of the slice: x: 4, y: 4, z: 8 (z_hi: 2, z_lo: 4; z = z_hi * 4 + z_lo), core: 2. Of those that a mesh axis runs over, the one named last changes fastest.
Arguments:
- inputs: bfloat16 [4, 16384, 4096], P('dp', 'ctx'), may hold values from -16 to 16
- value_weight: bfloat16 [4096, 512], P('ctx'), may hold values from -0.09375 to 0.09375
- query_states: bfloat16 [4, 16384, 2048], P('dp', 'ctx'), may hold values from -40 to 40
- key_states: bfloat16 [4, 16384, 512], P('dp', 'ctx'), may hold values from -6 to 6
- value_states: bfloat16 [4, 16384, 512], P('dp', 'ctx'), may hold values from -6 to 6
- attention_out: bfloat16 [4, 16384, 2048], P('dp', 'ctx'), may hold values from -4 to 4
- out_grad: bfloat16 [4, 16384, 2048], P('dp', 'ctx'), may hold values from -6 to 6
- segment_ids: int32 [4, 16384], P('dp', 'ctx'), may hold values from 0 to 31, never falling along the last dimension, each value on 1 to 4096 neighbouring positions
Outputs:
- query_grad: bfloat16 [4, 16384, 2048], P('dp', 'ctx')
- key_grad: bfloat16 [4, 16384, 512], P('dp', 'ctx')
- input_grad: bfloat16 [4, 16384, 4096], P('dp', 'ctx')
- weight_grad: float32 [4096, 512], P('ctx')
The draws below stay inside these ranges and needn't reach their ends.
Inputs may be any that keep to these rules, and one draw needn't show every extreme that they name: `segment_ids`: along each sequence the ids never fall; each record holds 1 to 4096 tokens and one holds exactly 4096.
All inputs are finite; a program needn't handle non-finite values.
Results may differ from the reference program's by a relative error of at most 0.0057.
Values may be sent and summed in bfloat16 or wider, within the bound.
A program may use at most 128 MiB of HBM per device.

```python
import math
import jax
import jax.numpy as jnp
import numpy as np
from jax import lax

D = 4096
HQ = 16
KVH = 4
DH = 128
W = 2048
TOK_DEV = 256
SPAN = 8
TOKENS = 16384
SEQS = 4
RECORDS = 32
MOST = 4096


def shared_draw(key):
    shape_kv = (SEQS, TOKENS, KVH, DH)
    drawn_rows = jax.random.truncated_normal(jax.random.fold_in(key, 11), -6.0, 6.0, shape_kv, jnp.float32)
    return drawn_rows


def draw_key_states(key, part):
    drawn_rows = shared_draw(key)
    return drawn_rows.reshape(SEQS, TOKENS, KVH * DH).astype(jnp.bfloat16)


def draw_query_states(key, part):
    group_size = HQ // KVH
    shape_q = (SEQS, TOKENS, KVH, group_size, DH)
    own_rows = jax.random.truncated_normal(jax.random.fold_in(key, 21), -6.0, 6.0, shape_q, jnp.float32)
    return own_rows.reshape(SEQS, TOKENS, HQ * DH).astype(jnp.bfloat16)


def raised(entries, rng, source, target, parts, factor):
    def block_of(axis_at):
        return (jnp.arange(entries.shape[axis_at]) // (entries.shape[axis_at] // parts)).reshape((-1,) + (1,) * (entries.ndim - 1 - axis_at))

    one_side = jax.random.permutation(rng, parts)[block_of(target)]
    far = (block_of(target) + parts // 2) % parts
    return jnp.where((block_of(source) == one_side) | (block_of(source) == far), factor * entries, entries)


def levels(own_key, shape, shards, smallest, top_value):
    level = 1.0
    for axis_at, parts in shards:
        heights = jax.random.uniform(jax.random.fold_in(jax.random.fold_in(own_key, 6), axis_at), (parts,), jnp.float32, smallest / len(shards), top_value / len(shards))
        level = level * jnp.repeat(jnp.exp(heights), shape[axis_at] // parts).reshape((-1,) + (1,) * (len(shape) - 1 - axis_at))
    return level


def profile(count, total, reach, slope):
    portions = [(1 << 20) // math.isqrt(grade ** slope) + 1 for grade in range(2, count + 1)]
    spare, given = total - reach - (count - 1), [1] * (count - 1)
    while spare > 0:
        movable = [i for i in range(count - 1) if given[i] < reach]
        pool, remaining = sum([portions[i] for i in movable]), spare
        for i in movable:
            addition = min(reach - given[i], max(1, remaining * portions[i] // pool), spare)
            given[i] = given[i] + addition
            spare = spare - addition
    return np.array([reach] + given)


def ragged(own_key, number_of, total, bound, skew):
    if number_of == 2:
        one = jax.random.randint(own_key, (), max(1, total - bound), min(bound, total - 1) + 1)
        return jnp.stack([one, total - one])
    lengths = jnp.asarray(profile(number_of, total, bound, skew), jnp.int32)
    twos = (number_of - 1) // 2
    donor, taker = lengths[1:1 + 2 * twos:2], lengths[2:2 + 2 * twos:2]
    margin = jnp.minimum(donor - 1, bound - taker)
    passed = jax.random.randint(jax.random.fold_in(own_key, 1), (twos,), 0, 1 << 20) % (margin + 1)
    lengths = lengths.at[1:1 + 2 * twos:2].set(donor - passed).at[2:2 + 2 * twos:2].set(taker + passed)
    return lengths[jax.random.permutation(jax.random.fold_in(own_key, 2), number_of)]


def gaussian(key, dims, spread, bound, pieces=(), held_as=jnp.bfloat16):
    array = spread * jax.random.normal(key, dims, jnp.float32)
    if pieces:
        array = array * levels(key, dims, pieces, -0.22, 0.18)
    return jnp.clip(array, -bound, bound).astype(held_as)


def bell_draw_with(key, shape, scale, limit, pieces, heavy, held_as=jnp.bfloat16):
    array = scale * jax.random.normal(key, shape, jnp.float32)
    if pieces:
        array = array * levels(key, shape, pieces, -0.22, 0.18)
    return jnp.clip(raised(array, jax.random.fold_in(key, 3), *heavy), -limit, limit).astype(held_as)


def setup_inputs(seed: int = 0) -> dict:
    streams_of = jax.random.split(jax.random.key(seed), 9)
    inputs = bell_draw_with(streams_of[0], (SEQS, TOKENS, D), 1.0, 16.0, ((0, 4), (1, 64)), (1, 2, 64, 4.0))
    value_weight = gaussian(streams_of[1], (D, KVH * DH), D ** -0.5, 0.09375, ((0, 64),))
    query_states = draw_query_states(jax.random.fold_in(streams_of[8], 71), 0)
    key_states = draw_key_states(jax.random.fold_in(streams_of[8], 71), 0)
    value_states = gaussian(streams_of[4], (SEQS, TOKENS, KVH * DH), 1.0, 6.0, ((0, 4), (1, 64)))
    attention_out = gaussian(streams_of[5], (SEQS, TOKENS, HQ * DH), 0.5, 4.0, ((0, 4), (1, 64)))
    out_grad = gaussian(streams_of[6], (SEQS, TOKENS, HQ * DH), 1.0, 6.0, ((0, 4), (1, 64)))
    segment_ids = jax.vmap(lambda own: jnp.searchsorted(jnp.cumsum(ragged(own, RECORDS, TOKENS, MOST, 2)), jnp.arange(TOKENS), side="right"))(jax.random.split(streams_of[7], SEQS)).reshape((SEQS, TOKENS)).astype(jnp.int32)
    return dict(inputs=inputs, value_weight=value_weight, query_states=query_states, key_states=key_states, value_states=value_states, attention_out=attention_out, out_grad=out_grad, segment_ids=segment_ids)


def record_starts(segment_ids):
    length = segment_ids.shape[0]
    position = jnp.arange(length, dtype=jnp.int32)
    begins = jnp.concatenate([jnp.ones((1,), dtype=jnp.bool_), segment_ids[1:] != segment_ids[:-1]])
    return lax.cummax(jnp.where(begins, position, jnp.zeros_like(position)), axis=0)

def attend_block(query_rows, key_rows, value_rows, grad_rows, output_rows, live_mask):
    factor = 1.0 / math.sqrt(DH)
    scores = jnp.einsum('rhgd,khd->hgrk', query_rows, key_rows) * factor
    scores = jnp.where(live_mask[None, None], scores, -1e+30)
    row_max = lax.optimization_barrier(jnp.max(scores, axis=-1, keepdims=True))
    exp_score = jnp.exp(scores - row_max)
    prob_full = exp_score / lax.optimization_barrier(jnp.sum(exp_score, axis=-1, keepdims=True))
    prob_low = lax.optimization_barrier(prob_full.astype(jnp.bfloat16)).astype(jnp.float32)
    row_delta = lax.optimization_barrier(jnp.sum(grad_rows * output_rows, axis=-1))
    prob_grad = jnp.einsum('rhgd,khd->hgrk', grad_rows, value_rows)
    score_grad = prob_full * (prob_grad - jnp.transpose(row_delta, (1, 2, 0))[..., None])
    score_grad = lax.optimization_barrier(score_grad.astype(jnp.bfloat16)).astype(jnp.float32)
    query_part = jnp.einsum('hgrk,khd->rhgd', score_grad, key_rows) * factor
    key_part = jnp.einsum('hgrk,rhgd->khd', score_grad, query_rows) * factor
    value_part = jnp.einsum('hgrk,rhgd->khd', prob_low, grad_rows)
    return (query_part, key_part, value_part)

def one_sequence(inputs, value_weight, query_states, key_states, value_states, attention_out, out_grad, segment_ids):
    starts = record_starts(segment_ids)
    group_size = HQ // KVH
    width_kv = KVH * DH
    span_rows = SPAN * TOK_DEV
    window_rows = span_rows + TOK_DEV
    pad_zero = jnp.zeros((span_rows, width_kv), jnp.float32)
    key_pad = jnp.concatenate([pad_zero, key_states.astype(jnp.float32)], axis=0)
    value_pad = jnp.concatenate([pad_zero, value_states.astype(jnp.float32)], axis=0)

    def block_step(carry, block_index):
        key_acc, value_acc = carry
        first_row = (block_index * TOK_DEV).astype(jnp.int32)
        query_rows = lax.dynamic_slice_in_dim(query_states, first_row, TOK_DEV, 0).astype(jnp.float32)
        query_rows = query_rows.reshape(TOK_DEV, KVH, group_size, DH)
        grad_rows = lax.dynamic_slice_in_dim(out_grad, first_row, TOK_DEV, 0).astype(jnp.float32)
        grad_rows = grad_rows.reshape(TOK_DEV, KVH, group_size, DH)
        output_rows = lax.dynamic_slice_in_dim(attention_out, first_row, TOK_DEV, 0).astype(jnp.float32)
        output_rows = output_rows.reshape(TOK_DEV, KVH, group_size, DH)
        key_rows = lax.dynamic_slice_in_dim(key_pad, first_row, window_rows, 0).reshape(window_rows, KVH, DH)
        value_rows = lax.dynamic_slice_in_dim(value_pad, first_row, window_rows, 0).reshape(window_rows, KVH, DH)
        query_pos = first_row + jnp.arange(TOK_DEV, dtype=jnp.int32)
        key_pos = first_row - span_rows + jnp.arange(window_rows, dtype=jnp.int32)
        query_start = lax.dynamic_slice_in_dim(starts, first_row, TOK_DEV, 0)
        live_mask = (key_pos[None, :] >= query_start[:, None]) & (key_pos[None, :] <= query_pos[:, None]) & (key_pos[None, :] > query_pos[:, None] - W)
        query_part, key_part, value_part = attend_block(query_rows, key_rows, value_rows, grad_rows, output_rows, live_mask)
        key_old = lax.dynamic_slice_in_dim(key_acc, first_row, window_rows, 0)
        key_acc = lax.dynamic_update_slice_in_dim(key_acc, key_old + key_part.reshape(window_rows, width_kv), first_row, 0)
        value_old = lax.dynamic_slice_in_dim(value_acc, first_row, window_rows, 0)
        value_acc = lax.dynamic_update_slice_in_dim(value_acc, value_old + value_part.reshape(window_rows, width_kv), first_row, 0)
        return ((key_acc, value_acc), query_part.reshape(TOK_DEV, HQ * DH).astype(jnp.bfloat16))
    zero_acc = jnp.zeros((TOKENS + span_rows, width_kv), jnp.float32)
    (key_acc, value_acc), query_grad = lax.scan(block_step, (zero_acc, zero_acc), jnp.arange(TOKENS // TOK_DEV, dtype=jnp.int32))
    query_grad = query_grad.reshape(TOKENS, HQ * DH)
    key_grad = key_acc[span_rows:].astype(jnp.bfloat16)
    value_delta = value_acc[span_rows:].astype(jnp.bfloat16)
    input_grad = jnp.dot(value_delta, value_weight.T, preferred_element_type=jnp.float32).astype(jnp.bfloat16)
    weight_part = jnp.dot(inputs.T, value_delta, preferred_element_type=jnp.float32)
    return (query_grad, key_grad, input_grad, weight_part)

def reference(inputs, value_weight, query_states, key_states, value_states, attention_out, out_grad, segment_ids):
    query_list = []
    key_list = []
    input_list = []
    weight_grad = jnp.zeros((D, KVH * DH), jnp.float32)
    for seq_index in range(SEQS):
        query_grad, key_grad, input_grad, weight_part = one_sequence(inputs[seq_index], value_weight, query_states[seq_index], key_states[seq_index], value_states[seq_index], attention_out[seq_index], out_grad[seq_index], segment_ids[seq_index])
        query_list.append(query_grad)
        key_list.append(key_grad)
        input_list.append(input_grad)
        weight_grad = weight_grad + weight_part
    return (jnp.stack(query_list), jnp.stack(key_list), jnp.stack(input_list), weight_grad)
```

```python
import math

import jax
import jax.numpy as jnp
from jax import lax
from jax.experimental import pallas as pl
from jax.experimental.pallas import tpu as pltpu
from jax.sharding import PartitionSpec as P

DH = 128
W = 2048
T = 256
CHIP = 2 * T
NK = W // T + 1
WIN = W + CHIP
FACTOR = 1.0 / math.sqrt(DH)
FACTOR2 = FACTOR * math.log2(math.e)
BF = jnp.bfloat16
F32 = jnp.float32
MESH = pl.DeviceIdType.MESH
ANY = pl.BlockSpec(memory_space=pl.ANY)
VM = pl.BlockSpec(memory_space=pltpu.VMEM)
NT = (((1,), (1,)), ((), ()))
NN = (((1,), (0,)), ((), ()))
TN = (((0,), (0,)), ((), ()))


def dot(a, b, dims):
    return lax.dot_general(a, b, dims, preferred_element_type=F32)


def signal(sem, ctx):
    pl.semaphore_signal(sem, inc=1, device_id={"ctx": ctx}, device_id_type=MESH)


def remote(src, dst, send, recv, ctx):
    return pltpu.make_async_remote_copy(
        src_ref=src,
        dst_ref=dst,
        send_sem=send,
        recv_sem=recv,
        device_id={"ctx": ctx},
        device_id_type=MESH,
    )


def gather_kernel(
    q_in, do_in, de_in, k_in, v_in, sg_in, kv_zero, sg_none,
    q_out, do_out, de_out, kv_out, sg_out,
    lsem, psend, precv, asend, arecv, rsend, rrecv,
):
    me = lax.axis_index("ctx")
    core = lax.rem(me, 2)
    other = 1 - core
    y = lax.rem(me // 2, 4)
    partner = me + 1 - 2 * core
    row0 = me - 2 * y
    has_next = me < 56
    has_prev = me >= 8

    barrier = pltpu.get_barrier_semaphore()
    signal(barrier, partner)
    for k in (1, 2, 3):
        signal(barrier, row0 + 2 * lax.rem(y + k, 4))

    @pl.when(has_next)
    def _():
        signal(barrier, me + 8)

    @pl.when(has_prev)
    def _():
        signal(barrier, me - 8)

    pl.semaphore_wait(barrier, 4 + has_next.astype(jnp.int32) + has_prev.astype(jnp.int32))

    rows = pl.ds(pl.multiple_of(core * T, T), T)
    kv_rows = pl.ds(pl.multiple_of(W + core * T, T), T)

    def cols(c, n):
        return pl.ds(pl.multiple_of(c * n, n), n)

    pairs = (
        (lambda c: k_in.at[:, cols(c, 2 * DH)], kv_out.at[0, kv_rows, :]),
        (lambda c: v_in.at[:, cols(c, 2 * DH)], kv_out.at[1, kv_rows, :]),
        (lambda c: sg_in, sg_out.at[4, core]),
        (lambda c: q_in.at[:, cols(c, 8 * DH)], q_out.at[rows, :]),
        (lambda c: do_in.at[:, cols(c, 8 * DH)], do_out.at[rows, :]),
        (lambda c: de_in.at[c], de_out.at[core]),
    )
    swaps = [
        remote(src(other), dst, psend.at[i], precv.at[i], partner)
        for i, (src, dst) in enumerate(pairs)
    ]
    locals_ = [
        pltpu.make_async_copy(src(core), dst, lsem.at[i]) for i, (src, dst) in enumerate(pairs)
    ]
    for i in range(6):
        swaps[i].start()
        locals_[i].start()
    for i in range(3):
        locals_[i].wait()
        swaps[i].wait_recv()

    def slot(s):
        return kv_out.at[:, pl.ds(s * CHIP, CHIP), :], sg_out.at[s]

    own, first = slot(4), slot(0)
    ahead = [remote(own[i], first[i], asend.at[i], arecv.at[i], me + 8) for i in (0, 1)]

    @pl.when(has_next)
    def _():
        ahead[0].start()
        ahead[1].start()

    def along(k, src):
        to = row0 + 2 * lax.rem(y + k, 4)
        dst = slot(4 - k)
        return [
            remote(src[i], dst[i], rsend.at[k - 1, i], rrecv.at[k - 1, i], to) for i in (0, 1)
        ]

    for k in (1, 2, 3):

        @pl.when(y + k < 4)
        def _():
            for copy in along(k, own):
                copy.start()

    @pl.when(has_prev)
    def _():
        ahead[0].wait_recv()
        ahead[1].wait_recv()

    @pl.when(jnp.logical_not(has_prev))
    def _():
        fill = (
            pltpu.make_async_copy(kv_zero, first[0], lsem.at[6]),
            pltpu.make_async_copy(sg_none, first[1], lsem.at[7]),
        )
        for copy in fill:
            copy.start()
        for copy in fill:
            copy.wait()

    for k in (1, 2, 3):

        @pl.when(y + k >= 4)
        def _():
            for copy in along(k, first):
                copy.start()

    for k in (1, 2, 3):
        for copy in along(k, own):
            copy.wait()
    for i in range(3):
        swaps[i].wait_send()
    for i in range(3, 6):
        locals_[i].wait()
        swaps[i].wait()

    @pl.when(has_next)
    def _():
        ahead[0].wait_send()
        ahead[1].wait_send()


def gather(q, do, de, k, v, sg):
    dma = pltpu.SemaphoreType.DMA
    return pl.pallas_call(
        gather_kernel,
        in_specs=[ANY] * 8,
        out_specs=[ANY] * 5,
        out_shape=[
            jax.ShapeDtypeStruct((CHIP, 8 * DH), BF),
            jax.ShapeDtypeStruct((CHIP, 8 * DH), BF),
            jax.ShapeDtypeStruct((2, 8, T), F32),
            jax.ShapeDtypeStruct((2, WIN, 2 * DH), BF),
            jax.ShapeDtypeStruct((5, 2, 8, T), jnp.int32),
        ],
        scratch_shapes=[
            dma((8,)), dma((6,)), dma((6,)), dma((2,)), dma((2,)), dma((3, 2)), dma((3, 2)),
        ],
        compiler_params=pltpu.CompilerParams(collective_id=0, has_side_effects=True),
        name="window_gather",
    )(
        q, do, de, k, v, sg,
        jnp.zeros((2, CHIP, 2 * DH), BF),
        jnp.full((2, 8, T), -1, jnp.int32),
    )


def attend_kernel(
    q_ref, do_ref, de_ref, k_ref, v_ref, sq_ref, sk_ref, dq_ref, dk_ref, dv_ref, bias, s_ref, dk, dv
):
    g, h, t = pl.program_id(0), pl.program_id(1), pl.program_id(2)

    def rows(c):
        return pl.ds(pl.multiple_of(t * T + c * T, T), T)

    @pl.when((g == 0) & (h == 0))
    def _():
        for c in range(NK):
            kpos = lax.broadcasted_iota(jnp.int32, (T, T), 0) + (c * T - W)
            qpos = lax.broadcasted_iota(jnp.int32, (T, T), 1)
            sk = sk_ref[rows(c), :]
            sk = jnp.concatenate([sk, sk], axis=1)
            live = (sk == sq_ref[pl.ds(t, 1), :]) & (kpos <= qpos) & (kpos > qpos - W)
            bias[t, c] = jnp.where(live, 0.0, -1e30)

    @pl.when((h == 0) & (t == 0))
    def _():
        dk[...] = jnp.zeros_like(dk)
        dv[...] = jnp.zeros_like(dv)

    q, do = q_ref[...], do_ref[...]
    top = jnp.full((8, T), -1e30, F32)
    for c in range(NK):
        s = dot(k_ref[0, rows(c), :], q, NT) + bias[t, c]
        s_ref[c] = s
        top = jnp.maximum(top, jnp.max(s.reshape(T // 8, 8, T), axis=0))
    top = jnp.max(top, axis=0, keepdims=True)
    total = jnp.zeros((8, T), F32)
    for c in range(NK):
        e = jnp.exp2((s_ref[c] - top) * FACTOR2)
        s_ref[c] = e
        total = total + jnp.sum(e.reshape(T // 8, 8, T), axis=0)
    inverse = 1.0 / jnp.sum(total, axis=0, keepdims=True)
    delta = de_ref[t, pl.ds(g * 4 + h, 1), :]
    dq = jnp.zeros((T, DH), F32)
    for c in range(NK):
        p = s_ref[c] * inverse
        dv[rows(c), :] += dot(p.astype(BF), do, NN)
        dp = dot(v_ref[0, rows(c), :], do, NT)
        ds = (p * (dp - delta)).astype(BF)
        dk[rows(c), :] += dot(ds, q, NN)
        dq = dq + dot(ds, k_ref[0, rows(c), :], TN)
    dq_ref[...] = (dq * FACTOR).astype(BF)

    @pl.when((h == 3) & (t == 1))
    def _():
        dk_ref[...] = (dk[...] * FACTOR).astype(BF)
        dv_ref[...] = dv[...].astype(BF)


def attend(q, do, de, kv, sq, sk):
    heads = pl.BlockSpec((T, DH), lambda g, h, t: (t, g * 4 + h))
    window = pl.BlockSpec((WIN, DH), lambda g, h, t: (0, g))
    return pl.pallas_call(
        attend_kernel,
        grid=(2, 4, 2),
        in_specs=[
            heads,
            heads,
            pl.BlockSpec((2, 8, T), lambda g, h, t: (0, 0, 0)),
            pl.BlockSpec((1, WIN, DH), lambda g, h, t: (0, 0, g)),
            pl.BlockSpec((1, WIN, DH), lambda g, h, t: (1, 0, g)),
            pl.BlockSpec((2, T), lambda g, h, t: (0, 0)),
            pl.BlockSpec((WIN, 128), lambda g, h, t: (0, 0)),
        ],
        out_specs=[heads, window, window],
        out_shape=[
            jax.ShapeDtypeStruct((CHIP, 8 * DH), BF),
            jax.ShapeDtypeStruct((WIN, 2 * DH), BF),
            jax.ShapeDtypeStruct((WIN, 2 * DH), BF),
        ],
        scratch_shapes=[
            pltpu.VMEM((2, NK, T, T), F32),
            pltpu.VMEM((NK, T, T), F32),
            pltpu.VMEM((WIN, DH), F32),
            pltpu.VMEM((WIN, DH), F32),
        ],
        compiler_params=pltpu.CompilerParams(vmem_limit_bytes=48 << 20),
        cost_estimate=pl.CostEstimate(
            flops=12_000_000_000, bytes_accessed=9_000_000, transcendentals=9_400_000
        ),
        name="attend",
    )(q, do, de, kv, kv, sq, sk)


def scatter_kernel(
    dq_in, dk_in, dv_in,
    dq_out, dk_out, vd_out, vx_out,
    got, part, kept, ahead_buf, total,
    lsem, psend, precv, asend, arecv, rsend, rrecv, xsend, xrecv,
):
    me = lax.axis_index("ctx")
    core = lax.rem(me, 2)
    other = 1 - core
    y = lax.rem(me // 2, 4)
    x = lax.rem(me // 8, 4)
    partner = me + 1 - 2 * core
    row0 = me - 2 * y
    column0 = me - 8 * x
    has_next = me < 56
    has_prev = me >= 8

    def row_peer(k):
        return row0 + 2 * lax.rem(y + k, 4)

    def column_peer(k):
        return column0 + 8 * lax.rem(x + k, 4)

    barrier = pltpu.get_barrier_semaphore()
    signal(barrier, partner)
    for k in (1, 2, 3):
        signal(barrier, row_peer(k))
        signal(barrier, column_peer(k))
    far_next = (x == 3) & has_next
    far_prev = (x == 0) & has_prev

    @pl.when(far_next)
    def _():
        signal(barrier, me + 8)

    @pl.when(far_prev)
    def _():
        signal(barrier, me - 8)

    pl.semaphore_wait(barrier, 7 + far_next.astype(jnp.int32) + far_prev.astype(jnp.int32))

    def half(c):
        return pl.ds(pl.multiple_of(c * T, T), T)

    def cols(c, n):
        return pl.ds(pl.multiple_of(c * n, n), n)

    def slot(ref, s):
        return ref.at[pl.ds(s * CHIP, CHIP), :]

    grads = (dv_in, dk_in)
    sends = [
        [
            remote(slot(grads[j], 4 - k), got.at[j, k - 1], rsend.at[j, k - 1], rrecv.at[j, k - 1], row_peer(4 - k))
            for k in (1, 2, 3)
        ]
        for j in (0, 1)
    ]
    keeps = [
        [pltpu.make_async_copy(slot(grads[j], 4 * i), kept.at[j, i], lsem.at[j, i]) for i in (0, 1)]
        for j in (0, 1)
    ]
    for j in (0, 1):
        for copy in sends[j] + keeps[j]:
            copy.start()
    dq_swap = remote(dq_in.at[half(other), :], dq_out.at[:, cols(core, 8 * DH)], psend.at[2], precv.at[2], partner)
    dq_keep = pltpu.make_async_copy(dq_in.at[half(core), :], dq_out.at[:, cols(core, 8 * DH)], lsem.at[2, 0])
    dq_swap.start()
    dq_keep.start()

    aheads = [
        remote(part.at[j], ahead_buf.at[j], asend.at[j], arecv.at[j], me - 8) for j in (0, 1)
    ]
    tails = []
    for j in (0, 1):
        for copy in keeps[j]:
            copy.wait()
        for copy in sends[j]:
            copy.wait_recv()
        before = kept[j, 0].astype(F32)
        for k in (1, 2, 3):
            before = before + jnp.where(y + k >= 4, got[j, k - 1].astype(F32), 0.0)
        part[j] = before.astype(BF)

        @pl.when(has_prev)
        def _():
            aheads[j].start()

    for j in (0, 1):
        mine = kept[j, 1].astype(F32)
        for k in (1, 2, 3):
            mine = mine + jnp.where(y + k < 4, got[j, k - 1].astype(F32), 0.0)

        @pl.when(has_next)
        def _():
            aheads[j].wait_recv()

        @pl.when(jnp.logical_not(has_next))
        def _():
            ahead_buf[j] = jnp.zeros_like(ahead_buf[j])

        total[j] = (mine + ahead_buf[j].astype(F32)).astype(BF)
        out = (vd_out, dk_out)[j]
        swap = remote(total.at[j, half(other), :], out.at[:, cols(core, 2 * DH)], psend.at[j], precv.at[j], partner)
        keep = pltpu.make_async_copy(total.at[j, half(core), :], out.at[:, cols(core, 2 * DH)], lsem.at[2, 1 + j])
        now = [swap, keep]
        if j == 0:
            now += [
                remote(total.at[0], vx_out.at[k], xsend.at[k - 1], xrecv.at[k - 1], column_peer(k))
                for k in (1, 2, 3)
            ]
            now.append(pltpu.make_async_copy(total.at[0], vx_out.at[0], lsem.at[2, 3]))
        for copy in now:
            copy.start()
        tails += now
    for copy in tails + [dq_swap, dq_keep]:
        copy.wait()
    for j in (0, 1):
        for copy in sends[j]:
            copy.wait_send()

        @pl.when(has_prev)
        def _():
            aheads[j].wait_send()


def scatter(dq, dk, dv):
    dma = pltpu.SemaphoreType.DMA
    return pl.pallas_call(
        scatter_kernel,
        in_specs=[ANY] * 3,
        out_specs=[ANY] * 4,
        out_shape=[
            jax.ShapeDtypeStruct((T, 16 * DH), BF),
            jax.ShapeDtypeStruct((T, 4 * DH), BF),
            jax.ShapeDtypeStruct((T, 4 * DH), BF),
            jax.ShapeDtypeStruct((4, CHIP, 2 * DH), BF),
        ],
        scratch_shapes=[
            pltpu.VMEM((2, 3, CHIP, 2 * DH), BF),
            pltpu.VMEM((2, CHIP, 2 * DH), BF),
            pltpu.VMEM((2, 2, CHIP, 2 * DH), BF),
            pltpu.VMEM((2, CHIP, 2 * DH), BF),
            pltpu.VMEM((2, CHIP, 2 * DH), BF),
            dma((3, 4)), dma((3,)), dma((3,)), dma((2,)), dma((2,)),
            dma((2, 3)), dma((2, 3)), dma((3,)), dma((3,)),
        ],
        compiler_params=pltpu.CompilerParams(
            collective_id=1, has_side_effects=True, vmem_limit_bytes=32 << 20
        ),
        name="grad_scatter",
    )(dq, dk, dv)


def reduce_kernel(
    w_in, w_out, got, summed, far, rsend, rrecv, zsend, zrecv, lsem
):
    me = lax.axis_index("ctx")
    low = lax.axis_index("dp")
    core = lax.rem(me, 2)
    y = lax.rem(me // 2, 4)
    place = lax.rem(me, 32)
    z = (me // 32) * 4 + low
    row0 = me - 2 * y

    def row_peer(k):
        return row0 + 2 * lax.rem(y + k, 4)

    def z_peer(j, c):
        to = lax.rem(z + j, 8)
        return {"dp": lax.rem(to, 4), "ctx": (to // 4) * 32 + place - core + c}, to // 4

    barrier = pltpu.get_barrier_semaphore()
    for k in (1, 2, 3):
        signal(barrier, row_peer(k))
    for j in range(8):
        for i in (0, 1):
            if j or i:
                pl.semaphore_signal(
                    barrier,
                    inc=1,
                    device_id=z_peer(j, (core if i == 0 else 1 - core))[0],
                    device_id_type=MESH,
                )
    pl.semaphore_wait(barrier, 18)

    sends = [
        remote(w_in.at[:, lax.rem(y + k, 4)], got.at[k - 1], rsend.at[k - 1], rrecv.at[k - 1], row_peer(k))
        for k in (1, 2, 3)
    ]
    for copy in sends:
        copy.start()
    mine = pltpu.make_async_copy(w_in.at[:, y], got.at[3], lsem.at[0])
    mine.start()
    mine.wait()
    for copy in sends:
        copy.wait_recv()
    acc = got[3].astype(F32)
    for k in range(3):
        acc = acc + got[k].astype(F32)
    summed[...] = acc.astype(BF).reshape(2, 2, 64, 2 * DH)

    copies = []
    for j in range(8):
        for i in (0, 1):
            c = core if i == 0 else 1 - core
            peer, high = z_peer(j, c)
            src = summed.at[high, c]
            if j == 0 and i == 0:
                copies.append(pltpu.make_async_copy(src, far.at[0, 0], lsem.at[1]))
            else:
                copies.append(
                    pltpu.make_async_remote_copy(
                        src_ref=src,
                        dst_ref=far.at[i, j],
                        send_sem=zsend.at[i, j],
                        recv_sem=zrecv.at[i, j],
                        device_id=peer,
                        device_id_type=MESH,
                    )
                )
    for copy in copies:
        copy.start()
    for copy in copies:
        copy.wait()
    for copy in sends:
        copy.wait_send()
    same = far[0, 0].astype(F32)
    cross = far[1, 0].astype(F32)
    for j in range(1, 8):
        same = same + far[0, j].astype(F32)
        cross = cross + far[1, j].astype(F32)
    w_out[:, : 2 * DH] = jnp.where(core == 0, same, cross)
    w_out[:, 2 * DH :] = jnp.where(core == 0, cross, same)


def reduce_weight(part):
    dma = pltpu.SemaphoreType.DMA
    return pl.pallas_call(
        reduce_kernel,
        in_specs=[ANY],
        out_specs=VM,
        out_shape=jax.ShapeDtypeStruct((64, 4 * DH), F32),
        scratch_shapes=[
            pltpu.VMEM((4, 2, 128, 2 * DH), BF),
            pltpu.VMEM((2, 2, 64, 2 * DH), BF),
            pltpu.VMEM((2, 8, 64, 2 * DH), BF),
            dma((3,)), dma((3,)), dma((2, 8)), dma((2, 8)), dma((2,)),
        ],
        compiler_params=pltpu.CompilerParams(collective_id=2, has_side_effects=True),
        name="weight_reduce",
    )(part)


def gathered_inputs(rows):
    me = lax.axis_index("ctx")
    x = lax.rem(me // 8, 4)
    strips = rows.reshape(T, 2, 4, 512)

    def strip(k):
        return lax.dynamic_index_in_dim(strips, lax.rem(x + k, 4), 2, keepdims=False).reshape(T, 1024)

    def along(k):
        return [(i, i - (i // 8 % 4) * 8 + ((i // 8 + k) % 4) * 8) for i in range(64)]

    got = [strip(0)] + [lax.ppermute(strip(k), "ctx", along(k)) for k in (1, 2, 3)]
    mine = jnp.concatenate(got, axis=0)
    return mine, lax.ppermute(mine, "ctx", [(i, i ^ 1) for i in range(64)])


def on_device(
    inputs, value_weight, query_states, key_states, value_states, attention_out, out_grad, segment_ids
):
    core = lax.rem(lax.axis_index("ctx"), 2)
    weight = lax.all_gather(value_weight, "ctx", axis=0, tiled=True)
    x_mine, x_other = gathered_inputs(inputs[0])
    delta = jnp.sum(
        (out_grad[0].astype(F32) * attention_out[0].astype(F32)).reshape(T, 16, DH), axis=-1
    )
    delta = delta.T.reshape(2, 8, T)
    seg = jnp.broadcast_to(segment_ids, (8, T))
    q, do, de, kv, sg = gather(
        query_states[0], out_grad[0], delta, key_states[0], value_states[0], seg
    )
    ids = sg[:, :, 0, :]
    dq, dk, dv = attend(
        q, do, de, kv, ids[4], jnp.broadcast_to(ids.reshape(WIN, 1), (WIN, 128))
    )
    query_grad, key_grad, value_delta, value_rows = scatter(dq, dk, dv)
    value_rows = value_rows.reshape(4, 2, T, 2 * DH)
    v_mine = lax.dynamic_index_in_dim(value_rows, core, 1, keepdims=False).reshape(4 * T, 2 * DH)
    v_other = lax.dynamic_index_in_dim(value_rows, 1 - core, 1, keepdims=False).reshape(4 * T, 2 * DH)
    part = (dot(x_mine, v_mine, TN) + dot(x_other, v_other, TN)).astype(BF)
    weight_grad = reduce_weight(part.reshape(2, 4, 128, 2 * DH))
    input_grad = dot(value_delta, weight, NT).astype(BF)
    return (query_grad[None], key_grad[None], input_grad[None], weight_grad)


def solution(mesh):
    placed = (
        P("dp", "ctx", None),
        P("ctx", None),
        P("dp", "ctx", None),
        P("dp", "ctx", None),
        P("dp", "ctx", None),
        P("dp", "ctx", None),
        P("dp", "ctx", None),
        P("dp", "ctx"),
    )
    return jax.shard_map(
        on_device,
        mesh=mesh,
        in_specs=placed,
        out_specs=(
            P("dp", "ctx", None),
            P("dp", "ctx", None),
            P("dp", "ctx", None),
            P("ctx", None),
        ),
        check_vma=False,
    )
```

```python
import math

import jax
import jax.numpy as jnp
from jax import lax
from jax.experimental import pallas as pl
from jax.experimental.pallas import tpu as pltpu
from jax.sharding import PartitionSpec as P

DH = 128
W = 2048
T = 256
CHIP = 2 * T
NK = W // T + 1
WIN = W + CHIP
FACTOR = 1.0 / math.sqrt(DH)
FACTOR2 = FACTOR * math.log2(math.e)
BF = jnp.bfloat16
F32 = jnp.float32
MESH = pl.DeviceIdType.MESH
ANY = pl.BlockSpec(memory_space=pl.ANY)
VM = pl.BlockSpec(memory_space=pltpu.VMEM)
NT = (((1,), (1,)), ((), ()))
NN = (((1,), (0,)), ((), ()))
TN = (((0,), (0,)), ((), ()))


def dot(a, b, dims):
    return lax.dot_general(a, b, dims, preferred_element_type=F32)


def signal(sem, ctx):
    pl.semaphore_signal(sem, inc=1, device_id={"ctx": ctx}, device_id_type=MESH)


def remote(src, dst, send, recv, ctx):
    return pltpu.make_async_remote_copy(
        src_ref=src,
        dst_ref=dst,
        send_sem=send,
        recv_sem=recv,
        device_id={"ctx": ctx},
        device_id_type=MESH,
    )


def gather_kernel(
    q_in, do_in, de_in, k_in, v_in, sg_in, kv_zero, sg_none,
    q_out, do_out, de_out, kv_out, sg_out,
    lsem, psend, precv, asend, arecv, rsend, rrecv,
):
    me = lax.axis_index("ctx")
    core = lax.rem(me, 2)
    other = 1 - core
    y = lax.rem(me // 2, 4)
    partner = me + 1 - 2 * core
    row0 = me - 2 * y
    has_next = me < 56
    has_prev = me >= 8

    barrier = pltpu.get_barrier_semaphore()
    signal(barrier, partner)
    for k in (1, 2, 3):
        signal(barrier, row0 + 2 * lax.rem(y + k, 4))

    @pl.when(has_next)
    def _():
        signal(barrier, me + 8)

    @pl.when(has_prev)
    def _():
        signal(barrier, me - 8)

    pl.semaphore_wait(barrier, 4 + has_next.astype(jnp.int32) + has_prev.astype(jnp.int32))

    rows = pl.ds(pl.multiple_of(core * T, T), T)
    kv_rows = pl.ds(pl.multiple_of(W + core * T, T), T)

    def cols(c, n):
        return pl.ds(pl.multiple_of(c * n, n), n)

    pairs = (
        (lambda c: k_in.at[:, cols(c, 2 * DH)], kv_out.at[0, kv_rows, :]),
        (lambda c: v_in.at[:, cols(c, 2 * DH)], kv_out.at[1, kv_rows, :]),
        (lambda c: sg_in, sg_out.at[4, core]),
        (lambda c: q_in.at[:, cols(c, 8 * DH)], q_out.at[rows, :]),
        (lambda c: do_in.at[:, cols(c, 8 * DH)], do_out.at[rows, :]),
        (lambda c: de_in.at[c], de_out.at[core]),
    )
    swaps = [
        remote(src(other), dst, psend.at[i], precv.at[i], partner)
        for i, (src, dst) in enumerate(pairs)
    ]
    locals_ = [
        pltpu.make_async_copy(src(core), dst, lsem.at[i]) for i, (src, dst) in enumerate(pairs)
    ]
    for i in range(6):
        swaps[i].start()
        locals_[i].start()
    for i in range(3):
        locals_[i].wait()
        swaps[i].wait_recv()

    def slot(s):
        return kv_out.at[:, pl.ds(s * CHIP, CHIP), :], sg_out.at[s]

    own, first = slot(4), slot(0)
    ahead = [remote(own[i], first[i], asend.at[i], arecv.at[i], me + 8) for i in (0, 1)]

    @pl.when(has_next)
    def _():
        ahead[0].start()
        ahead[1].start()

    def along(k, src):
        to = row0 + 2 * lax.rem(y + k, 4)
        dst = slot(4 - k)
        return [
            remote(src[i], dst[i], rsend.at[k - 1, i], rrecv.at[k - 1, i], to) for i in (0, 1)
        ]

    for k in (1, 2, 3):

        @pl.when(y + k < 4)
        def _():
            for copy in along(k, own):
                copy.start()

    @pl.when(has_prev)
    def _():
        ahead[0].wait_recv()
        ahead[1].wait_recv()

    @pl.when(jnp.logical_not(has_prev))
    def _():
        fill = (
            pltpu.make_async_copy(kv_zero, first[0], lsem.at[6]),
            pltpu.make_async_copy(sg_none, first[1], lsem.at[7]),
        )
        for copy in fill:
            copy.start()
        for copy in fill:
            copy.wait()

    for k in (1, 2, 3):

        @pl.when(y + k >= 4)
        def _():
            for copy in along(k, first):
                copy.start()

    for k in (1, 2, 3):
        for copy in along(k, own):
            copy.wait()
    for i in range(3):
        swaps[i].wait_send()
    for i in range(3, 6):
        locals_[i].wait()
        swaps[i].wait()

    @pl.when(has_next)
    def _():
        ahead[0].wait_send()
        ahead[1].wait_send()


def gather(q, do, de, k, v, sg):
    dma = pltpu.SemaphoreType.DMA
    return pl.pallas_call(
        gather_kernel,
        in_specs=[ANY] * 8,
        out_specs=[ANY] * 5,
        out_shape=[
            jax.ShapeDtypeStruct((CHIP, 8 * DH), BF),
            jax.ShapeDtypeStruct((CHIP, 8 * DH), BF),
            jax.ShapeDtypeStruct((2, 8, T), F32),
            jax.ShapeDtypeStruct((2, WIN, 2 * DH), BF),
            jax.ShapeDtypeStruct((5, 2, 8, T), jnp.int32),
        ],
        scratch_shapes=[
            dma((8,)), dma((6,)), dma((6,)), dma((2,)), dma((2,)), dma((3, 2)), dma((3, 2)),
        ],
        compiler_params=pltpu.CompilerParams(collective_id=0, has_side_effects=True),
        name="window_gather",
    )(
        q, do, de, k, v, sg,
        jnp.zeros((2, CHIP, 2 * DH), BF),
        jnp.full((2, 8, T), -1, jnp.int32),
    )


def attend_kernel(
    q_ref, do_ref, de_ref, k_ref, v_ref, sq_ref, sk_ref, x_in,
    dq_ref, dk_ref, dv_ref, xg,
    bias, s_ref, dk, dv, lsem, xsend, xrecv, fsend, frecv,
):
    g, h, t = pl.program_id(0), pl.program_id(1), pl.program_id(2)
    step = (g * 4 + h) * 2 + t
    me = lax.axis_index("ctx")
    core = lax.rem(me, 2)
    x = lax.rem(me // 8, 4)
    partner = me + 1 - 2 * core

    def column_peer(k):
        return me - 8 * x + 8 * lax.rem(x + k, 4)

    def strip(k, high):
        start = pl.multiple_of(high * 2048 + lax.rem(x + k, 4) * 512, 512)
        return x_in.at[:, pl.ds(start, 512)]

    stays = [
        pltpu.make_async_copy(strip(0, i), xg.at[core, 0, i], lsem.at[i]) for i in (0, 1)
    ]
    along = [
        remote(strip(k, i), xg.at[core, k, i], xsend.at[k - 1, i], xrecv.at[k - 1, i], column_peer(k))
        for k in (1, 2, 3)
        for i in (0, 1)
    ]
    forward = [
        remote(xg.at[core, k], xg.at[core, k], fsend.at[k], frecv.at[k], partner) for k in range(4)
    ]

    @pl.when(step == 0)
    def _():
        barrier = pltpu.get_barrier_semaphore()
        signal(barrier, partner)
        for k in (1, 2, 3):
            signal(barrier, column_peer(k))
        pl.semaphore_wait(barrier, 4)
        for copy in stays + along:
            copy.start()

    @pl.when(step == 11)
    def _():
        for copy in stays:
            copy.wait()
        for copy in along:
            copy.wait_recv()
        for copy in forward:
            copy.start()

    @pl.when(step == 15)
    def _():
        for copy in along:
            copy.wait_send()
        for copy in forward:
            copy.wait()

    def rows(c):
        return pl.ds(pl.multiple_of(t * T + c * T, T), T)

    @pl.when((g == 0) & (h == 0))
    def _():
        for c in range(NK):
            kpos = lax.broadcasted_iota(jnp.int32, (T, T), 0) + (c * T - W)
            qpos = lax.broadcasted_iota(jnp.int32, (T, T), 1)
            sk = sk_ref[rows(c), :]
            sk = jnp.concatenate([sk, sk], axis=1)
            live = (sk == sq_ref[pl.ds(t, 1), :]) & (kpos <= qpos) & (kpos > qpos - W)
            bias[t, c] = jnp.where(live, 0.0, -1e30)

    @pl.when((h == 0) & (t == 0))
    def _():
        dk[...] = jnp.zeros_like(dk)
        dv[...] = jnp.zeros_like(dv)

    q, do = q_ref[...], do_ref[...]
    top = jnp.full((8, T), -1e30, F32)
    for c in range(NK):
        s = dot(k_ref[0, rows(c), :], q, NT) + bias[t, c]
        s_ref[c] = s
        top = jnp.maximum(top, jnp.max(s.reshape(T // 8, 8, T), axis=0))
    top = jnp.max(top, axis=0, keepdims=True)
    total = jnp.zeros((8, T), F32)
    for c in range(NK):
        e = jnp.exp2((s_ref[c] - top) * FACTOR2)
        s_ref[c] = e
        total = total + jnp.sum(e.reshape(T // 8, 8, T), axis=0)
    inverse = 1.0 / jnp.sum(total, axis=0, keepdims=True)
    delta = de_ref[t, pl.ds(g * 4 + h, 1), :]
    dq = jnp.zeros((T, DH), F32)
    for c in range(NK):
        p = s_ref[c] * inverse
        dv[rows(c), :] += dot(p.astype(BF), do, NN)
        dp = dot(v_ref[0, rows(c), :], do, NT)
        ds = (p * (dp - delta)).astype(BF)
        dk[rows(c), :] += dot(ds, q, NN)
        dq = dq + dot(ds, k_ref[0, rows(c), :], TN)
    dq_ref[...] = (dq * FACTOR).astype(BF)

    @pl.when((h == 3) & (t == 1))
    def _():
        dk_ref[...] = (dk[...] * FACTOR).astype(BF)
        dv_ref[...] = dv[...].astype(BF)


def attend(q, do, de, kv, sq, sk, x):
    dma = pltpu.SemaphoreType.DMA
    heads = pl.BlockSpec((T, DH), lambda g, h, t: (t, g * 4 + h))
    window = pl.BlockSpec((WIN, DH), lambda g, h, t: (0, g))
    return pl.pallas_call(
        attend_kernel,
        grid=(2, 4, 2),
        in_specs=[
            heads,
            heads,
            pl.BlockSpec((2, 8, T), lambda g, h, t: (0, 0, 0)),
            pl.BlockSpec((1, WIN, DH), lambda g, h, t: (0, 0, g)),
            pl.BlockSpec((1, WIN, DH), lambda g, h, t: (1, 0, g)),
            pl.BlockSpec((2, T), lambda g, h, t: (0, 0)),
            pl.BlockSpec((WIN, 128), lambda g, h, t: (0, 0)),
            ANY,
        ],
        out_specs=[heads, window, window, ANY],
        out_shape=[
            jax.ShapeDtypeStruct((CHIP, 8 * DH), BF),
            jax.ShapeDtypeStruct((WIN, 2 * DH), BF),
            jax.ShapeDtypeStruct((WIN, 2 * DH), BF),
            jax.ShapeDtypeStruct((2, 4, 2, T, 512), BF),
        ],
        scratch_shapes=[
            pltpu.VMEM((2, NK, T, T), F32),
            pltpu.VMEM((NK, T, T), F32),
            pltpu.VMEM((WIN, DH), F32),
            pltpu.VMEM((WIN, DH), F32),
            dma((2,)), dma((3, 2)), dma((3, 2)), dma((4,)), dma((4,)),
        ],
        compiler_params=pltpu.CompilerParams(
            collective_id=3, has_side_effects=True, vmem_limit_bytes=40 << 20
        ),
        cost_estimate=pl.CostEstimate(
            flops=12_000_000_000, bytes_accessed=9_000_000, transcendentals=9_400_000
        ),
        name="attend",
    )(q, do, de, kv, kv, sq, sk, x)


def scatter_kernel(
    dq_in, dk_in, dv_in,
    dq_out, dk_out, vd_out, vx_out,
    got, part, kept, ahead_buf, total,
    lsem, psend, precv, asend, arecv, rsend, rrecv, xsend, xrecv,
):
    me = lax.axis_index("ctx")
    core = lax.rem(me, 2)
    other = 1 - core
    y = lax.rem(me // 2, 4)
    x = lax.rem(me // 8, 4)
    partner = me + 1 - 2 * core
    row0 = me - 2 * y
    column0 = me - 8 * x
    has_next = me < 56
    has_prev = me >= 8

    def row_peer(k):
        return row0 + 2 * lax.rem(y + k, 4)

    def column_peer(k):
        return column0 + 8 * lax.rem(x + k, 4)

    barrier = pltpu.get_barrier_semaphore()
    signal(barrier, partner)
    for k in (1, 2, 3):
        signal(barrier, row_peer(k))
        signal(barrier, column_peer(k))
    far_next = (x == 3) & has_next
    far_prev = (x == 0) & has_prev

    @pl.when(far_next)
    def _():
        signal(barrier, me + 8)

    @pl.when(far_prev)
    def _():
        signal(barrier, me - 8)

    pl.semaphore_wait(barrier, 7 + far_next.astype(jnp.int32) + far_prev.astype(jnp.int32))

    def half(c):
        return pl.ds(pl.multiple_of(c * T, T), T)

    def cols(c, n):
        return pl.ds(pl.multiple_of(c * n, n), n)

    def slot(ref, s):
        return ref.at[pl.ds(s * CHIP, CHIP), :]

    grads = (dv_in, dk_in)
    sends = [
        [
            remote(slot(grads[j], 4 - k), got.at[j, k - 1], rsend.at[j, k - 1], rrecv.at[j, k - 1], row_peer(4 - k))
            for k in (1, 2, 3)
        ]
        for j in (0, 1)
    ]
    keeps = [
        [pltpu.make_async_copy(slot(grads[j], 4 * i), kept.at[j, i], lsem.at[j, i]) for i in (0, 1)]
        for j in (0, 1)
    ]
    for j in (0, 1):
        for copy in sends[j] + keeps[j]:
            copy.start()
    dq_swap = remote(dq_in.at[half(other), :], dq_out.at[:, cols(core, 8 * DH)], psend.at[2], precv.at[2], partner)
    dq_keep = pltpu.make_async_copy(dq_in.at[half(core), :], dq_out.at[:, cols(core, 8 * DH)], lsem.at[2, 0])
    dq_swap.start()
    dq_keep.start()

    aheads = [
        remote(part.at[j], ahead_buf.at[j], asend.at[j], arecv.at[j], me - 8) for j in (0, 1)
    ]
    tails = []
    for j in (0, 1):
        for copy in keeps[j]:
            copy.wait()
        for copy in sends[j]:
            copy.wait_recv()
        before = kept[j, 0].astype(F32)
        for k in (1, 2, 3):
            before = before + jnp.where(y + k >= 4, got[j, k - 1].astype(F32), 0.0)
        part[j] = before.astype(BF)

        @pl.when(has_prev)
        def _():
            aheads[j].start()

    for j in (0, 1):
        mine = kept[j, 1].astype(F32)
        for k in (1, 2, 3):
            mine = mine + jnp.where(y + k < 4, got[j, k - 1].astype(F32), 0.0)

        @pl.when(has_next)
        def _():
            aheads[j].wait_recv()

        @pl.when(jnp.logical_not(has_next))
        def _():
            ahead_buf[j] = jnp.zeros_like(ahead_buf[j])

        total[j] = (mine + ahead_buf[j].astype(F32)).astype(BF).reshape(2, T, 2 * DH)
        out = (vd_out, dk_out)[j]
        swap = remote(total.at[j, other], out.at[:, cols(core, 2 * DH)], psend.at[j], precv.at[j], partner)
        keep = pltpu.make_async_copy(total.at[j, core], out.at[:, cols(core, 2 * DH)], lsem.at[2, 1 + j])
        now = [swap, keep]
        if j == 0:
            now += [
                remote(total.at[0], vx_out.at[:, k], xsend.at[k - 1], xrecv.at[k - 1], column_peer(k))
                for k in (1, 2, 3)
            ]
            now.append(pltpu.make_async_copy(total.at[0], vx_out.at[:, 0], lsem.at[2, 3]))
        for copy in now:
            copy.start()
        tails += now
    for copy in tails + [dq_swap, dq_keep]:
        copy.wait()
    for j in (0, 1):
        for copy in sends[j]:
            copy.wait_send()

        @pl.when(has_prev)
        def _():
            aheads[j].wait_send()


def scatter(dq, dk, dv):
    dma = pltpu.SemaphoreType.DMA
    return pl.pallas_call(
        scatter_kernel,
        in_specs=[ANY] * 3,
        out_specs=[ANY] * 4,
        out_shape=[
            jax.ShapeDtypeStruct((T, 16 * DH), BF),
            jax.ShapeDtypeStruct((T, 4 * DH), BF),
            jax.ShapeDtypeStruct((T, 4 * DH), BF),
            jax.ShapeDtypeStruct((2, 4, T, 2 * DH), BF),
        ],
        scratch_shapes=[
            pltpu.VMEM((2, 3, CHIP, 2 * DH), BF),
            pltpu.VMEM((2, CHIP, 2 * DH), BF),
            pltpu.VMEM((2, 2, CHIP, 2 * DH), BF),
            pltpu.VMEM((2, CHIP, 2 * DH), BF),
            pltpu.VMEM((2, 2, T, 2 * DH), BF),
            dma((3, 4)), dma((3,)), dma((3,)), dma((2,)), dma((2,)),
            dma((2, 3)), dma((2, 3)), dma((3,)), dma((3,)),
        ],
        compiler_params=pltpu.CompilerParams(
            collective_id=1, has_side_effects=True, vmem_limit_bytes=32 << 20
        ),
        name="grad_scatter",
    )(dq, dk, dv)


def reduce_kernel(
    xg, vx, vd, weight, w_out, in_out, part, got, summed, far, rsend, rrecv, zsend, zrecv, lsem
):
    me = lax.axis_index("ctx")
    low = lax.axis_index("dp")
    core = lax.rem(me, 2)
    y = lax.rem(me // 2, 4)
    place = lax.rem(me, 32)
    z = (me // 32) * 4 + low
    row0 = me - 2 * y

    def row_peer(k):
        return row0 + 2 * lax.rem(y + k, 4)

    def z_peer(j, c):
        to = lax.rem(z + j, 8)
        return {"dp": lax.rem(to, 4), "ctx": (to // 4) * 32 + place - core + c}, to // 4

    barrier = pltpu.get_barrier_semaphore()
    for k in (1, 2, 3):
        signal(barrier, row_peer(k))
    for j in range(8):
        for i in (0, 1):
            if j or i:
                pl.semaphore_signal(
                    barrier,
                    inc=1,
                    device_id=z_peer(j, (core if i == 0 else 1 - core))[0],
                    device_id_type=MESH,
                )
    pl.semaphore_wait(barrier, 18)

    for i in (0, 1):
        acc = jnp.zeros((512, 2 * DH), F32)
        for a in (0, 1):
            for k in range(4):
                acc = acc + dot(xg[a, k, i], vx[a, k], TN)
        part[i] = acc.astype(BF).reshape(4, 128, 2 * DH)

    sends = [
        remote(part.at[:, lax.rem(y + k, 4)], got.at[k - 1], rsend.at[k - 1], rrecv.at[k - 1], row_peer(k))
        for k in (1, 2, 3)
    ]
    for copy in sends:
        copy.start()
    for i in range(8):
        in_out[:, i * 512 : (i + 1) * 512] = dot(
            vd[...], weight[i * 512 : (i + 1) * 512, :], NT
        ).astype(BF)
    for copy in sends:
        copy.wait_recv()
    acc = part[:, y].astype(F32)
    for k in range(3):
        acc = acc + got[k].astype(F32)
    summed[...] = acc.astype(BF).reshape(2, 2, 64, 2 * DH)

    copies = []
    for j in range(8):
        for i in (0, 1):
            c = core if i == 0 else 1 - core
            peer, high = z_peer(j, c)
            src = summed.at[high, c]
            if j == 0 and i == 0:
                copies.append(pltpu.make_async_copy(src, far.at[0, 0], lsem))
            else:
                copies.append(
                    pltpu.make_async_remote_copy(
                        src_ref=src,
                        dst_ref=far.at[i, j],
                        send_sem=zsend.at[i, j],
                        recv_sem=zrecv.at[i, j],
                        device_id=peer,
                        device_id_type=MESH,
                    )
                )
    for copy in copies:
        copy.start()
    for copy in copies:
        copy.wait()
    for copy in sends:
        copy.wait_send()
    same = far[0, 0].astype(F32)
    cross = far[1, 0].astype(F32)
    for j in range(1, 8):
        same = same + far[0, j].astype(F32)
        cross = cross + far[1, j].astype(F32)
    w_out[:, : 2 * DH] = jnp.where(core == 0, same, cross)
    w_out[:, 2 * DH :] = jnp.where(core == 0, cross, same)


def reduce_weight(xg, vx, vd, weight):
    dma = pltpu.SemaphoreType.DMA
    return pl.pallas_call(
        reduce_kernel,
        in_specs=[VM] * 4,
        out_specs=[VM, VM],
        out_shape=[
            jax.ShapeDtypeStruct((64, 4 * DH), F32),
            jax.ShapeDtypeStruct((T, 4096), BF),
        ],
        scratch_shapes=[
            pltpu.VMEM((2, 4, 128, 2 * DH), BF),
            pltpu.VMEM((3, 2, 128, 2 * DH), BF),
            pltpu.VMEM((2, 2, 64, 2 * DH), BF),
            pltpu.VMEM((2, 8, 64, 2 * DH), BF),
            dma((3,)), dma((3,)), dma((2, 8)), dma((2, 8)), dma,
        ],
        compiler_params=pltpu.CompilerParams(
            collective_id=2, has_side_effects=True, vmem_limit_bytes=32 << 20
        ),
        name="weight_reduce",
    )(xg, vx, vd, weight)


def on_device(
    inputs, value_weight, query_states, key_states, value_states, attention_out, out_grad, segment_ids
):
    weight = lax.all_gather(value_weight, "ctx", axis=0, tiled=True)
    delta = jnp.sum(
        (out_grad[0].astype(F32) * attention_out[0].astype(F32)).reshape(T, 16, DH), axis=-1
    )
    delta = delta.T.reshape(2, 8, T)
    seg = jnp.broadcast_to(segment_ids, (8, T))
    q, do, de, kv, sg = gather(
        query_states[0], out_grad[0], delta, key_states[0], value_states[0], seg
    )
    ids = sg[:, :, 0, :]
    dq, dk, dv, xg = attend(
        q, do, de, kv, ids[4], jnp.broadcast_to(ids.reshape(WIN, 1), (WIN, 128)), inputs[0]
    )
    query_grad, key_grad, value_delta, value_rows = scatter(dq, dk, dv)
    weight_grad, input_grad = reduce_weight(xg, value_rows, value_delta, weight)
    return (query_grad[None], key_grad[None], input_grad[None], weight_grad)


def solution(mesh):
    placed = (
        P("dp", "ctx", None),
        P("ctx", None),
        P("dp", "ctx", None),
        P("dp", "ctx", None),
        P("dp", "ctx", None),
        P("dp", "ctx", None),
        P("dp", "ctx", None),
        P("dp", "ctx"),
    )
    return jax.shard_map(
        on_device,
        mesh=mesh,
        in_specs=placed,
        out_specs=(
            P("dp", "ctx", None),
            P("dp", "ctx", None),
            P("dp", "ctx", None),
            P("ctx", None),
        ),
        check_vma=False,
    )
```

```python
import math

import jax
import jax.numpy as jnp
from jax import lax
from jax.experimental import pallas as pl
from jax.experimental.pallas import tpu as pltpu
from jax.sharding import PartitionSpec as P

DH = 128
W = 2048
T = 256
CHIP = 2 * T
NK = W // T + 1
WIN = W + CHIP
FACTOR = 1.0 / math.sqrt(DH)
FACTOR2 = FACTOR * math.log2(math.e)
BF = jnp.bfloat16
F32 = jnp.float32
MESH = pl.DeviceIdType.MESH
ANY = pl.BlockSpec(memory_space=pl.ANY)
VM = pl.BlockSpec(memory_space=pltpu.VMEM)
NT = (((1,), (1,)), ((), ()))
NN = (((1,), (0,)), ((), ()))
TN = (((0,), (0,)), ((), ()))


def dot(a, b, dims):
    return lax.dot_general(a, b, dims, preferred_element_type=F32)


def signal(sem, ctx):
    pl.semaphore_signal(sem, inc=1, device_id={"ctx": ctx}, device_id_type=MESH)


def remote(src, dst, send, recv, ctx):
    return pltpu.make_async_remote_copy(
        src_ref=src,
        dst_ref=dst,
        send_sem=send,
        recv_sem=recv,
        device_id={"ctx": ctx},
        device_id_type=MESH,
    )


def main_kernel(
    q_in, do_in, o_in, k_in, v_in, sg_in, x_in,
    dq_out, vd_out, vx_out, dk_out, xg,
    q_s, do_s, o_s, kv, sg, bias, s_ref, p_ref, acc, dq_s, dvp, dkp, got, part, ahead, total,
    lsem, psend, precv, asend, arecv, rsend, rrecv, gsend, grecv, hsend, hrecv,
    vsend, vrecv, xsend, xrecv, fsend, frecv,
):
    me = lax.axis_index("ctx")
    core = lax.rem(me, 2)
    other = 1 - core
    y = lax.rem(me // 2, 4)
    x = lax.rem(me // 8, 4)
    partner = me + 1 - 2 * core
    has_next = me < 56
    has_prev = me >= 8
    far_next = (x == 3) & has_next
    far_prev = (x == 0) & has_prev

    def row_peer(k):
        return me - 2 * y + 2 * lax.rem(y + k, 4)

    def column_peer(k):
        return me - 8 * x + 8 * lax.rem(x + k, 4)

    barrier = pltpu.get_barrier_semaphore()
    signal(barrier, partner)
    for k in (1, 2, 3):
        signal(barrier, row_peer(k))
        signal(barrier, column_peer(k))

    @pl.when(far_next)
    def _():
        signal(barrier, me + 8)

    @pl.when(far_prev)
    def _():
        signal(barrier, me - 8)

    sg[4, core] = jnp.broadcast_to(sg_in[...], (8, T))

    @pl.when(jnp.logical_not(has_prev))
    def _():
        kv[:, :CHIP, :] = jnp.zeros((4, CHIP, DH), BF)
        sg[0] = jnp.full((2, 8, T), -1, jnp.int32)

    pl.semaphore_wait(barrier, 7 + far_next.astype(jnp.int32) + far_prev.astype(jnp.int32))

    half = pl.ds(pl.multiple_of(core * T, T), T)
    rest = pl.ds(pl.multiple_of(other * T, T), T)
    home = pl.ds(pl.multiple_of(W + core * T, T), T)

    def cols(start, n):
        return pl.ds(pl.multiple_of(start * n, n), n)

    def source(i, c):
        if i < 4:
            return (k_in, v_in)[i // 2].at[:, cols(c * 2 + i % 2, DH)]
        return (q_in, do_in, o_in)[i - 4].at[:, cols(c, 8 * DH)]

    def target(i):
        if i < 4:
            return kv.at[i, home, :]
        return (q_s, do_s, o_s)[i - 4].at[half, :]

    swaps = [remote(source(i, other), target(i), psend.at[i], precv.at[i], partner) for i in range(7)]
    stays = [pltpu.make_async_copy(source(i, core), target(i), lsem.at[i]) for i in range(7)]
    sg_swap = remote(sg.at[4, core], sg.at[4, core], psend.at[7], precv.at[7], partner)

    def both(i):
        stays[i].start()
        swaps[i].start()

    both(0)
    sg_swap.start()
    for i in (4, 5, 1, 2, 3, 6):
        both(i)

    def block(u, s):
        if u == 4:
            return sg.at[s]
        return kv.at[u, pl.ds(s * CHIP, CHIP), :]

    def forth(u):
        return remote(block(u, 4), block(u, 0), asend.at[u], arecv.at[u], me + 8)

    def along(u, k, s):
        return remote(
            block(u, s), block(u, 4 - k), rsend.at[u, k - 1], rrecv.at[u, k - 1], row_peer(k)
        )

    def send_own(u):
        if u == 4:
            sg_swap.wait_recv()
        else:
            stays[u].wait()
            swaps[u].wait_recv()

        @pl.when(has_next)
        def _():
            forth(u).start()

        for k in (1, 2, 3):

            @pl.when(y + k < 4)
            def _():
                along(u, k, 4).start()

    def relay(u):
        @pl.when(has_prev)
        def _():
            forth(u).wait_recv()

        for k in (1, 2, 3):

            @pl.when(y + k >= 4)
            def _():
                along(u, k, 0).start()

    def arrived(u):
        for k in (1, 2, 3):
            along(u, k, 4).wait_recv()

    send_own(4)
    send_own(0)
    relay(4)
    relay(0)
    for i in (4, 5):
        stays[i].wait()
        swaps[i].wait_recv()
    arrived(4)

    for i in range(NK + 1):
        sk = jnp.transpose(sg[i // 2, i % 2].astype(F32))[:, :1]
        sk = jnp.broadcast_to(sk, (T, T))
        for t in (0, 1):
            c = i - t
            if 0 <= c < NK:
                live = sk == sg[4, t][:1, :].astype(F32)
                kpos = lax.broadcasted_iota(jnp.int32, (T, T), 0)
                qpos = lax.broadcasted_iota(jnp.int32, (T, T), 1)
                if c == 0:
                    live = live & (kpos > qpos)
                if c == NK - 1:
                    live = live & (kpos <= qpos)
                bias[t, c] = jnp.where(live, 0.0, -1e30)
    arrived(0)

    def give(g, k):
        return remote(
            dvp.at[g, pl.ds((4 - k) * CHIP, CHIP), :],
            got.at[g, k - 1],
            gsend.at[g, k - 1],
            grecv.at[g, k - 1],
            row_peer(4 - k),
        )

    def back(g):
        return remote(part.at[g], ahead.at[g], hsend.at[g], hrecv.at[g], me - 8)

    def give_start(g):
        for k in (1, 2, 3):
            give(g, k).start()

    def give_sum(g):
        for k in (1, 2, 3):
            give(g, k).wait_recv()
        before = dvp[g, :CHIP, :].astype(F32)
        for k in (1, 2, 3):
            before = before + jnp.where(y + k >= 4, got[g, k - 1].astype(F32), 0.0)
        part[g] = before.astype(BF)

        @pl.when(has_prev)
        def _():
            back(g).start()

    def spread(g):
        return [
            remote(
                total.at[g],
                vx_out.at[:, k, :, pl.ds(g * DH, DH)],
                vsend.at[g, k - 1],
                vrecv.at[g, k - 1],
                column_peer(k),
            )
            for k in (1, 2, 3)
        ] + [
            remote(
                total.at[g, other],
                vd_out.at[:, cols(core * 2 + g, DH)],
                psend.at[8 + g],
                precv.at[8 + g],
                partner,
            )
        ]

    def keep(g):
        return [
            pltpu.make_async_copy(total.at[g], vx_out.at[:, 0, :, pl.ds(g * DH, DH)], lsem.at[8 + g]),
            pltpu.make_async_copy(
                total.at[g, core], vd_out.at[:, cols(core * 2 + g, DH)], lsem.at[10 + g]
            ),
        ]

    def give_total(g):
        @pl.when(has_next)
        def _():
            back(g).wait_recv()

        @pl.when(jnp.logical_not(has_next))
        def _():
            ahead[g] = jnp.zeros((CHIP, DH), BF)

        mine = dvp[g, W:, :].astype(F32) + ahead[g].astype(F32)
        for k in (1, 2, 3):
            mine = mine + jnp.where(y + k < 4, got[g, k - 1].astype(F32), 0.0)
        total[g] = mine.astype(BF).reshape(2, T, DH)
        for copy in spread(g) + keep(g):
            copy.start()

    def strip(k, high):
        start = pl.multiple_of(high * 2048 + lax.rem(x + k, 4) * 512, 512)
        return x_in.at[:, pl.ds(start, 512)]

    def x_keep():
        return [pltpu.make_async_copy(strip(0, i), xg.at[core, 0, i], lsem.at[12 + i]) for i in (0, 1)]

    def x_along():
        return [
            remote(
                strip(k, i), xg.at[core, k, i], xsend.at[k - 1, i], xrecv.at[k - 1, i], column_peer(k)
            )
            for k in (1, 2, 3)
            for i in (0, 1)
        ]

    def x_forward():
        return [
            remote(xg.at[core, k], xg.at[core, k], fsend.at[k], frecv.at[k], partner) for k in range(4)
        ]

    def at(n, when, *calls):
        @pl.when(n == when)
        def _():
            for f, *args in calls:
                f(*args)

    def start_all(make):
        for copy in make():
            copy.start()

    def x_pass():
        for copy in x_keep():
            copy.wait()
        for copy in x_along():
            copy.wait_recv()
        for copy in x_forward():
            copy.start()

    def rows(t, c):
        return pl.ds(pl.multiple_of(t * T + c * T, T), T)

    def phase1(n, _):
        g, h, t = n // 8, lax.rem(n // 2, 4), lax.rem(n, 2)
        at(n, 0, (send_own, 1))
        at(n, 3, (relay, 1), (send_own, 2))
        at(n, 8, (arrived, 1), (relay, 2), (send_own, 3), (give_start, 0))
        at(n, 12, (relay, 3), (start_all, x_keep), (start_all, x_along))

        @pl.when(lax.rem(n, 8) == 0)
        def _():
            acc[...] = jnp.zeros_like(acc)

        head = pl.ds(pl.multiple_of((g * 4 + h) * DH, DH), DH)
        here = pl.ds(pl.multiple_of(t * T, T), T)
        q, do = q_s[here, head], do_s[here, head]
        top = jnp.full((8, T), -1e30, F32)
        for c in range(NK):
            s = dot(kv[g, rows(t, c), :], q, NT) + bias[t, c]
            s_ref[c] = s
            top = jnp.maximum(top, jnp.max(s.reshape(T // 8, 8, T), axis=0))
        top = jnp.max(top, axis=0, keepdims=True)
        weight = jnp.zeros((8, T), F32)
        for c in range(NK):
            e = jnp.exp2((s_ref[c] - top) * FACTOR2)
            s_ref[c] = e
            weight = weight + jnp.sum(e.reshape(T // 8, 8, T), axis=0)
        inverse = 1.0 / jnp.sum(weight, axis=0, keepdims=True)
        for c in range(NK):
            p = (s_ref[c] * inverse).astype(BF)
            p_ref[n, c] = p
            acc[rows(t, c), :] += dot(p, do, NN)

        @pl.when(lax.rem(n, 8) == 7)
        def _():
            dvp[g] = acc[...].astype(BF)

        return 0

    lax.fori_loop(0, 16, phase1, 0)

    def dq_swap(g):
        block = pl.ds(g * 4 * DH, 4 * DH)
        place = cols(core * 2 + g, 4 * DH)
        return [
            remote(dq_s.at[rest, block], dq_out.at[:, place], psend.at[10 + g], precv.at[10 + g], partner),
            pltpu.make_async_copy(dq_s.at[half, block], dq_out.at[:, place], lsem.at[14 + g]),
        ]

    stays[6].wait()
    swaps[6].wait_recv()
    give_start(1)
    arrived(2)

    def phase2(n, _):
        g, h, t = n // 8, lax.rem(n // 2, 4), lax.rem(n, 2)
        at(n, 1, (give_sum, 0))
        at(n, 4, (give_total, 0), (give_sum, 1))
        at(n, 6, (x_pass,))
        at(n, 8, (arrived, 3), (start_all, lambda: dq_swap(0)))
        at(n, 10, (give_total, 1))

        @pl.when(lax.rem(n, 8) == 0)
        def _():
            acc[...] = jnp.zeros_like(acc)

        head = pl.ds(pl.multiple_of((g * 4 + h) * DH, DH), DH)
        here = pl.ds(pl.multiple_of(t * T, T), T)
        q, do = q_s[here, head], do_s[here, head]
        product = do.astype(F32) * o_s[here, head].astype(F32)
        delta = jnp.sum(jnp.transpose(product), axis=0, keepdims=True)
        dq = jnp.zeros((T, DH), F32)
        for c in range(NK):
            dp = dot(kv[2 + g, rows(t, c), :], do, NT)
            ds = (p_ref[n, c].astype(F32) * (dp - delta)).astype(BF)
            acc[rows(t, c), :] += dot(ds, q, NN)
            dq = dq + dot(ds, kv[g, rows(t, c), :], TN)
        dq_s[here, head] = (dq * FACTOR).astype(BF)

        @pl.when(lax.rem(n, 8) == 7)
        def _():
            dkp[g] = (acc[...] * FACTOR).astype(BF)

        return 0

    lax.fori_loop(0, 16, phase2, 0)

    dk_copy = pltpu.make_async_copy(dkp, dk_out, lsem.at[16])
    dk_copy.start()
    for copy in dq_swap(1):
        copy.start()
    dk_copy.wait()
    for g in (0, 1):
        for copy in dq_swap(g) + spread(g) + keep(g):
            copy.wait()
        for k in (1, 2, 3):
            give(g, k).wait_send()

        @pl.when(has_prev)
        def _():
            back(g).wait_send()

    for copy in x_along():
        copy.wait_send()
    for copy in x_forward():
        copy.wait()
    for i in range(7):
        swaps[i].wait_send()
    sg_swap.wait_send()
    for u in range(5):

        @pl.when(has_next)
        def _():
            forth(u).wait_send()

        for k in (1, 2, 3):
            along(u, k, 4).wait_send()


def attend(q, do, o, k, v, sg, x):
    dma = pltpu.SemaphoreType.DMA
    return pl.pallas_call(
        main_kernel,
        in_specs=[ANY] * 5 + [VM, ANY],
        out_specs=[ANY] * 5,
        out_shape=[
            jax.ShapeDtypeStruct((T, 16 * DH), BF),
            jax.ShapeDtypeStruct((T, 4 * DH), BF),
            jax.ShapeDtypeStruct((2, 4, T, 2 * DH), BF),
            jax.ShapeDtypeStruct((2, WIN, DH), BF),
            jax.ShapeDtypeStruct((2, 4, 2, T, 512), BF),
        ],
        scratch_shapes=[
            pltpu.VMEM((CHIP, 8 * DH), BF),
            pltpu.VMEM((CHIP, 8 * DH), BF),
            pltpu.VMEM((CHIP, 8 * DH), BF),
            pltpu.VMEM((4, WIN, DH), BF),
            pltpu.VMEM((5, 2, 8, T), jnp.int32),
            pltpu.VMEM((2, NK, T, T), F32),
            pltpu.VMEM((NK, T, T), F32),
            pltpu.VMEM((16, NK, T, T), BF),
            pltpu.VMEM((WIN, DH), F32),
            pltpu.VMEM((CHIP, 8 * DH), BF),
            pltpu.VMEM((2, WIN, DH), BF),
            pltpu.VMEM((2, WIN, DH), BF),
            pltpu.VMEM((2, 3, CHIP, DH), BF),
            pltpu.VMEM((2, CHIP, DH), BF),
            pltpu.VMEM((2, CHIP, DH), BF),
            pltpu.VMEM((2, 2, T, DH), BF),
            dma((17,)), dma((12,)), dma((12,)), dma((5,)), dma((5,)), dma((5, 3)), dma((5, 3)),
            dma((2, 3)), dma((2, 3)), dma((2,)), dma((2,)),
            dma((2, 3)), dma((2, 3)), dma((3, 2)), dma((3, 2)), dma((4,)), dma((4,)),
        ],
        compiler_params=pltpu.CompilerParams(
            collective_id=0, has_side_effects=True, vmem_limit_bytes=56 << 20
        ),
        cost_estimate=pl.CostEstimate(
            flops=12_000_000_000, bytes_accessed=20_000_000, transcendentals=9_400_000
        ),
        name="attend",
    )(q, do, o, k, v, sg, x)


def finish_kernel(
    xg_in, vx_in, vd_in, w_in, dk_in,
    w_out, in_out, dk_out,
    xg, vx, vd, weight, part, got, summed, far, kgot, kept, kpart, kahead, ktotal,
    lsem, rsend, rrecv, zsend, zrecv, gsend, grecv, hsend, hrecv, psend, precv,
):
    me = lax.axis_index("ctx")
    low = lax.axis_index("dp")
    core = lax.rem(me, 2)
    other = 1 - core
    y = lax.rem(me // 2, 4)
    x = lax.rem(me // 8, 4)
    place = lax.rem(me, 32)
    z = (me // 32) * 4 + low
    partner = me + 1 - 2 * core
    has_next = me < 56
    has_prev = me >= 8

    def row_peer(k):
        return me - 2 * y + 2 * lax.rem(y + k, 4)

    def z_peer(j, c):
        to = lax.rem(z + j, 8)
        return {"dp": lax.rem(to, 4), "ctx": (to // 4) * 32 + place - core + c}, to // 4

    near_next = has_next
    near_prev = has_prev

    barrier = pltpu.get_barrier_semaphore()
    for k in (1, 2, 3):
        signal(barrier, row_peer(k))
    for j in range(8):
        for i in (0, 1):
            if j or i:
                pl.semaphore_signal(
                    barrier,
                    inc=1,
                    device_id=z_peer(j, (core if i == 0 else other))[0],
                    device_id_type=MESH,
                )

    @pl.when(near_next)
    def _():
        signal(barrier, me + 8)

    @pl.when(near_prev)
    def _():
        signal(barrier, me - 8)

    loads = [
        pltpu.make_async_copy(a, b, lsem.at[i])
        for i, (a, b) in enumerate(((vx_in, vx), (xg_in, xg), (vd_in, vd), (w_in, weight)))
    ]
    for copy in loads:
        copy.start()
    keeps = [
        pltpu.make_async_copy(dk_in.at[:, pl.ds(i * W, CHIP), :], kept.at[i], lsem.at[4 + i])
        for i in (0, 1)
    ]
    for copy in keeps:
        copy.start()
    pl.semaphore_wait(barrier, 18 + near_next.astype(jnp.int32) + near_prev.astype(jnp.int32))

    gives = [
        remote(
            dk_in.at[:, pl.ds((4 - k) * CHIP, CHIP), :],
            kgot.at[k - 1],
            gsend.at[k - 1],
            grecv.at[k - 1],
            row_peer(4 - k),
        )
        for k in (1, 2, 3)
    ]
    loads[0].wait()
    loads[1].wait()
    for i in (0, 1):
        acc = jnp.zeros((512, 2 * DH), F32)
        for a in (0, 1):
            for k in range(4):
                acc = acc + dot(xg[a, k, i], vx[a, k], TN)
        part[i] = acc.astype(BF).reshape(4, 128, 2 * DH)
    sends = [
        remote(part.at[:, lax.rem(y + k, 4)], got.at[k - 1], rsend.at[k - 1], rrecv.at[k - 1], row_peer(k))
        for k in (1, 2, 3)
    ]
    for copy in sends + gives:
        copy.start()
    loads[2].wait()
    loads[3].wait()
    for i in range(8):
        in_out[:, i * 512 : (i + 1) * 512] = dot(
            vd[...], weight[i * 512 : (i + 1) * 512, :], NT
        ).astype(BF)
    for copy in sends:
        copy.wait_recv()
    acc = part[:, y].astype(F32)
    for k in range(3):
        acc = acc + got[k].astype(F32)
    summed[...] = acc.astype(BF).reshape(2, 2, 64, 2 * DH)

    copies = []
    for j in range(8):
        for i in (0, 1):
            c = core if i == 0 else other
            peer, high = z_peer(j, c)
            src = summed.at[high, c]
            if j == 0 and i == 0:
                copies.append(pltpu.make_async_copy(src, far.at[0, 0], lsem.at[6]))
            else:
                copies.append(
                    pltpu.make_async_remote_copy(
                        src_ref=src,
                        dst_ref=far.at[i, j],
                        send_sem=zsend.at[i, j],
                        recv_sem=zrecv.at[i, j],
                        device_id=peer,
                        device_id_type=MESH,
                    )
                )
    for copy in copies:
        copy.start()

    for copy in keeps:
        copy.wait()
    for copy in gives:
        copy.wait_recv()
    before = kept[0].astype(F32)
    mine = kept[1].astype(F32)
    for k in (1, 2, 3):
        before = before + jnp.where(y + k >= 4, kgot[k - 1].astype(F32), 0.0)
        mine = mine + jnp.where(y + k < 4, kgot[k - 1].astype(F32), 0.0)
    kpart[...] = before.astype(BF)
    back = remote(kpart, kahead, hsend, hrecv, me - 8)

    @pl.when(has_prev)
    def _():
        back.start()

    for copy in copies:
        copy.wait()
    same = far[0, 0].astype(F32)
    cross = far[1, 0].astype(F32)
    for j in range(1, 8):
        same = same + far[0, j].astype(F32)
        cross = cross + far[1, j].astype(F32)
    w_out[:, : 2 * DH] = jnp.where(core == 0, same, cross)
    w_out[:, 2 * DH :] = jnp.where(core == 0, cross, same)

    @pl.when(has_next)
    def _():
        back.wait_recv()

    @pl.when(jnp.logical_not(has_next))
    def _():
        kahead[...] = jnp.zeros_like(kahead)

    ktotal[...] = (mine + kahead[...].astype(F32)).astype(BF).reshape(2, 2, T, DH)
    swaps = []
    for g in (0, 1):
        columns = pl.ds(pl.multiple_of((core * 2 + g) * DH, DH), DH)
        swaps += [
            remote(ktotal.at[g, other], dk_out.at[:, columns], psend.at[g], precv.at[g], partner),
            pltpu.make_async_copy(ktotal.at[g, core], dk_out.at[:, columns], lsem.at[7 + g]),
        ]
    for copy in swaps:
        copy.start()
    for copy in swaps:
        copy.wait()
    for copy in sends + gives:
        copy.wait_send()

    @pl.when(has_prev)
    def _():
        back.wait_send()


def finish(xg, vx, vd, weight, dk):
    dma = pltpu.SemaphoreType.DMA
    return pl.pallas_call(
        finish_kernel,
        in_specs=[ANY] * 5,
        out_specs=[VM, VM, VM],
        out_shape=[
            jax.ShapeDtypeStruct((64, 4 * DH), F32),
            jax.ShapeDtypeStruct((T, 4096), BF),
            jax.ShapeDtypeStruct((T, 4 * DH), BF),
        ],
        scratch_shapes=[
            pltpu.VMEM((2, 4, 2, T, 512), BF),
            pltpu.VMEM((2, 4, T, 2 * DH), BF),
            pltpu.VMEM((T, 4 * DH), BF),
            pltpu.VMEM((4096, 4 * DH), BF),
            pltpu.VMEM((2, 4, 128, 2 * DH), BF),
            pltpu.VMEM((3, 2, 128, 2 * DH), BF),
            pltpu.VMEM((2, 2, 64, 2 * DH), BF),
            pltpu.VMEM((2, 8, 64, 2 * DH), BF),
            pltpu.VMEM((3, 2, CHIP, DH), BF),
            pltpu.VMEM((2, 2, CHIP, DH), BF),
            pltpu.VMEM((2, CHIP, DH), BF),
            pltpu.VMEM((2, CHIP, DH), BF),
            pltpu.VMEM((2, 2, T, DH), BF),
            dma((9,)), dma((3,)), dma((3,)), dma((2, 8)), dma((2, 8)),
            dma((3,)), dma((3,)), dma, dma, dma((2,)), dma((2,)),
        ],
        compiler_params=pltpu.CompilerParams(
            collective_id=1, has_side_effects=True, vmem_limit_bytes=40 << 20
        ),
        name="finish",
    )(xg, vx, vd, weight, dk)


def on_device(
    inputs, value_weight, query_states, key_states, value_states, attention_out, out_grad, segment_ids
):
    weight = lax.all_gather(value_weight, "ctx", axis=0, tiled=True)
    query_grad, value_delta, value_rows, dk, xg = attend(
        query_states[0],
        out_grad[0],
        attention_out[0],
        key_states[0],
        value_states[0],
        segment_ids,
        inputs[0],
    )
    weight_grad, input_grad, key_grad = finish(xg, value_rows, value_delta, weight, dk)
    return (query_grad[None], key_grad[None], input_grad[None], weight_grad)


def solution(mesh):
    placed = (
        P("dp", "ctx", None),
        P("ctx", None),
        P("dp", "ctx", None),
        P("dp", "ctx", None),
        P("dp", "ctx", None),
        P("dp", "ctx", None),
        P("dp", "ctx", None),
        P("dp", "ctx"),
    )
    return jax.shard_map(
        on_device,
        mesh=mesh,
        in_specs=placed,
        out_specs=(
            P("dp", "ctx", None),
            P("dp", "ctx", None),
            P("dp", "ctx", None),
            P("ctx", None),
        ),
        check_vma=False,
    )
```

```python
import math

import jax
import jax.numpy as jnp
from jax import lax
from jax.experimental import pallas as pl
from jax.experimental.pallas import tpu as pltpu
from jax.sharding import PartitionSpec as P

DH = 128
W = 2048
T = 256
CHIP = 2 * T
NK = W // T + 1
WIN = W + CHIP
FACTOR = 1.0 / math.sqrt(DH)
FACTOR2 = FACTOR * math.log2(math.e)
BF = jnp.bfloat16
F32 = jnp.float32
MESH = pl.DeviceIdType.MESH
ANY = pl.BlockSpec(memory_space=pl.ANY)
VM = pl.BlockSpec(memory_space=pltpu.VMEM)
NT = (((1,), (1,)), ((), ()))
NN = (((1,), (0,)), ((), ()))
TN = (((0,), (0,)), ((), ()))


def dot(a, b, dims):
    return lax.dot_general(a, b, dims, preferred_element_type=F32)


def signal(sem, ctx):
    pl.semaphore_signal(sem, inc=1, device_id={"ctx": ctx}, device_id_type=MESH)


def remote(src, dst, send, recv, ctx):
    return pltpu.make_async_remote_copy(
        src_ref=src,
        dst_ref=dst,
        send_sem=send,
        recv_sem=recv,
        device_id={"ctx": ctx},
        device_id_type=MESH,
    )


def main_kernel(
    q_in, do_in, o_in, k_in, v_in, sg_in, x_in, w_in,
    dq_out, dk_out, in_out, w_out, wg,
    q_s, do_s, o_s, kv, sg, bias, s_ref, p_ref, acc, dq_s, gp, got, part, ahead, total,
    vd, vx, xg, wpart, wgot, wsum, far, weight,
    lsem, psend, precv, asend, arecv, rsend, rrecv, gsend, grecv, hsend, hrecv,
    vsend, vrecv, xsend, xrecv, fsend, frecv, ysend, yrecv, zsend, zrecv, wsend, wrecv,
):
    me = lax.axis_index("ctx")
    core = lax.rem(me, 2)
    other = 1 - core
    y = lax.rem(me // 2, 4)
    x = lax.rem(me // 8, 4)
    partner = me + 1 - 2 * core
    has_next = me < 56
    has_prev = me >= 8
    low = lax.axis_index("dp")
    high = me // 32
    place = lax.rem(me, 32)
    far_next = (x == 3) & has_next
    far_prev = (x == 0) & has_prev

    def row_peer(k):
        return me - 2 * y + 2 * lax.rem(y + k, 4)

    def column_peer(k):
        return me - 8 * x + 8 * lax.rem(x + k, 4)

    def z_peer(j, c):
        to = lax.rem(high * 4 + low + j, 8)
        return {"dp": lax.rem(to, 4), "ctx": (to // 4) * 32 + place - core + c}, to // 4

    barrier = pltpu.get_barrier_semaphore()
    for j in range(8):
        for c in (core, other):
            if j or c is other:
                pl.semaphore_signal(
                    barrier, inc=1, device_id=z_peer(j, c)[0], device_id_type=MESH
                )
    for k in (1, 2, 3):
        signal(barrier, row_peer(k))
        signal(barrier, column_peer(k))

    @pl.when(far_next)
    def _():
        signal(barrier, me + 8)

    @pl.when(far_prev)
    def _():
        signal(barrier, me - 8)

    sg[4, core] = jnp.broadcast_to(sg_in[...], (8, T))

    @pl.when(jnp.logical_not(has_prev))
    def _():
        kv[:, :CHIP, :] = jnp.zeros((4, CHIP, DH), BF)
        sg[0] = jnp.full((2, 8, T), -1, jnp.int32)

    pl.semaphore_wait(barrier, 21 + far_next.astype(jnp.int32) + far_prev.astype(jnp.int32))

    half = pl.ds(pl.multiple_of(core * T, T), T)
    rest = pl.ds(pl.multiple_of(other * T, T), T)
    home = pl.ds(pl.multiple_of(W + core * T, T), T)

    def cols(start, n):
        return pl.ds(pl.multiple_of(start * n, n), n)

    def source(i, c):
        if i < 4:
            return (k_in, v_in)[i // 2].at[:, cols(c * 2 + i % 2, DH)]
        return (q_in, do_in, o_in)[i - 4].at[:, cols(c, 8 * DH)]

    def target(i):
        if i < 4:
            return kv.at[i, home, :]
        return (q_s, do_s, o_s)[i - 4].at[half, :]

    swaps = [remote(source(i, other), target(i), psend.at[i], precv.at[i], partner) for i in range(7)]
    stays = [pltpu.make_async_copy(source(i, core), target(i), lsem.at[i]) for i in range(7)]
    sg_swap = remote(sg.at[4, core], sg.at[4, core], psend.at[7], precv.at[7], partner)

    def both(i):
        stays[i].start()
        swaps[i].start()

    both(0)
    sg_swap.start()
    for i in (4, 5, 1, 2, 3, 6):
        both(i)

    def block(u, s):
        if u == 4:
            return sg.at[s]
        return kv.at[u, pl.ds(s * CHIP, CHIP), :]

    def forth(u):
        return remote(block(u, 4), block(u, 0), asend.at[u], arecv.at[u], me + 8)

    def along(u, k, s):
        return remote(
            block(u, s), block(u, 4 - k), rsend.at[u, k - 1], rrecv.at[u, k - 1], row_peer(k)
        )

    def send_own(u):
        if u == 4:
            sg_swap.wait_recv()
        else:
            stays[u].wait()
            swaps[u].wait_recv()

        @pl.when(has_next)
        def _():
            forth(u).start()

        for k in (1, 2, 3):

            @pl.when(y + k < 4)
            def _():
                along(u, k, 4).start()

    def relay(u):
        @pl.when(has_prev)
        def _():
            forth(u).wait_recv()

        for k in (1, 2, 3):

            @pl.when(y + k >= 4)
            def _():
                along(u, k, 0).start()

    def arrived(u):
        for k in (1, 2, 3):
            along(u, k, 4).wait_recv()

    send_own(4)
    send_own(0)
    relay(4)
    relay(0)
    for i in (4, 5):
        stays[i].wait()
        swaps[i].wait_recv()
    arrived(4)

    for i in range(NK + 1):
        sk = jnp.transpose(sg[i // 2, i % 2].astype(F32))[:, :1]
        sk = jnp.broadcast_to(sk, (T, T))
        for t in (0, 1):
            c = i - t
            if 0 <= c < NK:
                live = sk == sg[4, t][:1, :].astype(F32)
                kpos = lax.broadcasted_iota(jnp.int32, (T, T), 0)
                qpos = lax.broadcasted_iota(jnp.int32, (T, T), 1)
                if c == 0:
                    live = live & (kpos > qpos)
                if c == NK - 1:
                    live = live & (kpos <= qpos)
                bias[t, c] = jnp.where(live, 0.0, -1e30)
    arrived(0)

    w_stay = pltpu.make_async_copy(w_in, wg.at[high, x, y, core], lsem.at[17])
    w_swap = remote(w_in, wg.at[high, x, y, core], wsend.at[0], wrecv.at[0], partner)
    w_cross = remote(
        w_in,
        wg.at[high, x, y, core],
        wsend.at[1],
        wrecv.at[1 + core],
        (1 - high) * 32 + place - core + high,
    )

    def w_from(c):
        return remote(w_in, wg.at[high, x, y, c], wsend.at[1], wrecv.at[1 + c], partner)

    def w_x(k):
        return remote(
            wg.at[core, x, y], wg.at[core, x, y], wsend.at[1 + k], wrecv.at[2 + k], column_peer(k)
        )

    def w_y(k):
        return remote(
            wg.at[core, :, y], wg.at[core, :, y], wsend.at[4 + k], wrecv.at[5 + k], row_peer(k)
        )

    w_hand = remote(wg.at[core], wg.at[core], wsend.at[8], wrecv.at[9], partner)

    def w_begin():
        w_cross.start()

        @pl.when(core == high)
        def _():
            w_stay.start()

        @pl.when(core != high)
        def _():
            w_swap.start()

    def w_along_x():
        @pl.when(core == high)
        def _():
            w_stay.wait()
            w_swap.wait_recv()

        @pl.when(core != high)
        def _():
            w_swap.wait_send()
            w_from(0).wait_recv()
            w_from(1).wait_recv()

        for k in (1, 2, 3):
            w_x(k).start()

    def w_along_y():
        for k in (1, 2, 3):
            w_x(k).wait_recv()
        for k in (1, 2, 3):
            w_y(k).start()

    def w_across():
        for k in (1, 2, 3):
            w_y(k).wait_recv()
        w_hand.start()

    w_load = pltpu.make_async_copy(wg, weight, lsem.at[18])

    def w_done():
        w_hand.wait()
        w_cross.wait_send()
        for k in (1, 2, 3):
            w_x(k).wait_send()
            w_y(k).wait_send()
        w_load.start()

    def give(g, k):
        return remote(
            gp.at[g, pl.ds((4 - k) * CHIP, CHIP), :],
            got.at[g, k - 1],
            gsend.at[g, k - 1],
            grecv.at[g, k - 1],
            row_peer(4 - k),
        )

    def back(g):
        return remote(part.at[g], ahead.at[g], hsend.at[g], hrecv.at[g], me - 8)

    def give_start(g):
        for k in (1, 2, 3):
            give(g, k).start()

    def give_sum(g):
        for k in (1, 2, 3):
            give(g, k).wait_recv()
        before = gp[g, :CHIP, :].astype(F32)
        for k in (1, 2, 3):
            before = before + jnp.where(y + k >= 4, got[g, k - 1].astype(F32), 0.0)
        part[g] = before.astype(BF)

        @pl.when(has_prev)
        def _():
            back(g).start()

    def spread(u):
        g = u % 2
        columns = cols(core * 2 + g, DH)
        dst = vd if u < 2 else dk_out
        copies = [
            remote(total.at[u, other], dst.at[:, columns], psend.at[8 + u], precv.at[8 + u], partner)
        ]
        if u < 2:
            copies += [
                remote(
                    total.at[u],
                    vx.at[:, k, :, pl.ds(g * DH, DH)],
                    vsend.at[g, k - 1],
                    vrecv.at[g, k - 1],
                    column_peer(k),
                )
                for k in (1, 2, 3)
            ]
        return copies

    def keep(u):
        g = u % 2
        columns = cols(core * 2 + g, DH)
        if u < 2:
            return [
                pltpu.make_async_copy(total.at[u, core], vd.at[:, columns], lsem.at[8 + u]),
                pltpu.make_async_copy(total.at[u], vx.at[:, 0, :, pl.ds(g * DH, DH)], lsem.at[10 + u]),
            ]
        return [pltpu.make_async_copy(total.at[u, core], dk_out.at[:, columns], lsem.at[8 + u])]

    def give_total(g):
        @pl.when(has_next)
        def _():
            back(g).wait_recv()

        @pl.when(jnp.logical_not(has_next))
        def _():
            ahead[g] = jnp.zeros((CHIP, DH), BF)

        mine = gp[g, W:, :].astype(F32) + ahead[g].astype(F32)
        for k in (1, 2, 3):
            mine = mine + jnp.where(y + k < 4, got[g, k - 1].astype(F32), 0.0)
        total[g] = mine.astype(BF).reshape(2, T, DH)
        for copy in spread(g) + keep(g):
            copy.start()

    def strip(k, high):
        start = pl.multiple_of(high * 2048 + lax.rem(x + k, 4) * 512, 512)
        return x_in.at[:, pl.ds(start, 512)]

    def x_keep():
        return [pltpu.make_async_copy(strip(0, i), xg.at[core, 0, i], lsem.at[12 + i]) for i in (0, 1)]

    def x_along():
        return [
            remote(
                strip(k, i), xg.at[core, k, i], xsend.at[k - 1, i], xrecv.at[k - 1, i], column_peer(k)
            )
            for k in (1, 2, 3)
            for i in (0, 1)
        ]

    def x_forward():
        return [
            remote(xg.at[core, k], xg.at[core, k], fsend.at[k], frecv.at[k], partner) for k in range(4)
        ]

    def at(n, when, *calls):
        @pl.when(n == when)
        def _():
            for f, *args in calls:
                f(*args)

    def start_all(make):
        for copy in make():
            copy.start()

    def x_pass():
        for copy in x_keep():
            copy.wait()
        for copy in x_along():
            copy.wait_recv()
        for copy in x_forward():
            copy.start()

    def w_part():
        for copy in x_forward():
            copy.wait()
        for u in (0, 1):
            for copy in spread(u) + keep(u):
                copy.wait()
        for i in (0, 1):
            sums = jnp.zeros((512, 2 * DH), F32)
            for a in (0, 1):
                for k in range(4):
                    sums = sums + dot(xg[a, k, i], vx[a, k], TN)
            wpart[i] = sums.astype(BF).reshape(4, 128, 2 * DH)
        for copy in y_sends():
            copy.start()

    def y_sends():
        return [
            remote(
                wpart.at[:, lax.rem(y + k, 4)],
                wgot.at[k - 1],
                ysend.at[k - 1],
                yrecv.at[k - 1],
                row_peer(k),
            )
            for k in (1, 2, 3)
        ]

    def z_sends():
        copies = []
        for j in range(8):
            for i in (0, 1):
                peer, part_of = z_peer(j, core if i == 0 else other)
                src = wsum.at[part_of, core if i == 0 else other]
                if j == 0 and i == 0:
                    copies.append(pltpu.make_async_copy(src, far.at[0, 0], lsem.at[7]))
                else:
                    copies.append(
                        pltpu.make_async_remote_copy(
                            src_ref=src,
                            dst_ref=far.at[i, j],
                            send_sem=zsend.at[i, j],
                            recv_sem=zrecv.at[i, j],
                            device_id=peer,
                            device_id_type=MESH,
                        )
                    )
        return copies

    def w_sum():
        for copy in y_sends():
            copy.wait_recv()
        sums = wpart[:, y].astype(F32)
        for k in range(3):
            sums = sums + wgot[k].astype(F32)
        wsum[...] = sums.astype(BF).reshape(2, 2, 64, 2 * DH)
        for copy in z_sends():
            copy.start()

    def w_end():
        for copy in z_sends():
            copy.wait()
        for copy in y_sends():
            copy.wait_send()
        same = far[0, 0].astype(F32)
        cross = far[1, 0].astype(F32)
        for j in range(1, 8):
            same = same + far[0, j].astype(F32)
            cross = cross + far[1, j].astype(F32)
        w_out[:, : 2 * DH] = jnp.where(core == 0, same, cross)
        w_out[:, 2 * DH :] = jnp.where(core == 0, cross, same)

    def rows(t, c):
        return pl.ds(pl.multiple_of(t * T + c * T, T), T)

    def phase1(n, _):
        g, h, t = n // 8, lax.rem(n // 2, 4), lax.rem(n, 2)
        at(n, 0, (send_own, 1), (w_begin,))
        at(n, 3, (relay, 1), (send_own, 2), (w_along_x,), (start_all, x_keep), (start_all, x_along))
        at(n, 8, (arrived, 1), (relay, 2), (send_own, 3), (give_start, 0))
        at(n, 12, (relay, 3))

        @pl.when(lax.rem(n, 8) == 0)
        def _():
            acc[...] = jnp.zeros_like(acc)

        head = pl.ds(pl.multiple_of((g * 4 + h) * DH, DH), DH)
        here = pl.ds(pl.multiple_of(t * T, T), T)
        q, do = q_s[here, head], do_s[here, head]
        top = jnp.full((8, T), -1e30, F32)
        for c in range(NK):
            s = dot(kv[g, rows(t, c), :], q, NT) + bias[t, c]
            s_ref[c] = s
            top = jnp.maximum(top, jnp.max(s.reshape(T // 8, 8, T), axis=0))
        top = jnp.max(top, axis=0, keepdims=True)
        weight = jnp.zeros((8, T), F32)
        for c in range(NK):
            e = jnp.exp2((s_ref[c] - top) * FACTOR2)
            s_ref[c] = e
            weight = weight + jnp.sum(e.reshape(T // 8, 8, T), axis=0)
        inverse = 1.0 / jnp.sum(weight, axis=0, keepdims=True)
        for c in range(NK):
            p = (s_ref[c] * inverse).astype(BF)
            p_ref[n, c] = p
            acc[rows(t, c), :] += dot(p, do, NN)

        @pl.when(lax.rem(n, 8) == 7)
        def _():
            gp[g] = acc[...].astype(BF)

        return 0

    lax.fori_loop(0, 16, phase1, 0)

    def dq_swap(g):
        block = pl.ds(g * 4 * DH, 4 * DH)
        place = cols(core * 2 + g, 4 * DH)
        return [
            remote(dq_s.at[rest, block], dq_out.at[:, place], psend.at[12 + g], precv.at[12 + g], partner),
            pltpu.make_async_copy(dq_s.at[half, block], dq_out.at[:, place], lsem.at[14 + g]),
        ]

    stays[6].wait()
    swaps[6].wait_recv()
    give_start(1)
    arrived(2)

    def phase2(n, _):
        g, h, t = n // 8, lax.rem(n // 2, 4), lax.rem(n, 2)
        at(n, 1, (give_sum, 0))
        at(n, 4, (give_total, 0), (give_sum, 1))
        at(n, 5, (x_pass,), (w_along_y,))
        at(n, 8, (arrived, 3), (give_start, 2))
        at(n, 9, (give_total, 1))
        at(n, 13, (give_sum, 2))

        @pl.when(lax.rem(n, 8) == 0)
        def _():
            acc[...] = jnp.zeros_like(acc)

        head = pl.ds(pl.multiple_of((g * 4 + h) * DH, DH), DH)
        here = pl.ds(pl.multiple_of(t * T, T), T)
        q, do = q_s[here, head], do_s[here, head]
        product = do.astype(F32) * o_s[here, head].astype(F32)
        delta = jnp.sum(jnp.transpose(product), axis=0, keepdims=True)
        for c in range(NK):
            dp = dot(kv[2 + g, rows(t, c), :], do, NT)
            ds = (p_ref[n, c].astype(F32) * (dp - delta)).astype(BF)
            p_ref[n, c] = ds
            acc[rows(t, c), :] += dot(ds, q, NN)

        @pl.when(lax.rem(n, 8) == 7)
        def _():
            gp[2 + g] = (acc[...] * FACTOR).astype(BF)

        return 0

    lax.fori_loop(0, 16, phase2, 0)
    give_start(3)
    w_across()
    w_part()

    def phase3(n, _):
        g, h, t = n // 8, lax.rem(n // 2, 4), lax.rem(n, 2)
        at(n, 3, (give_total, 2))
        at(n, 6, (w_sum,))
        at(n, 8, (start_all, lambda: dq_swap(0)))
        at(n, 10, (give_sum, 3))
        dq = jnp.zeros((T, DH), F32)
        for c in range(NK):
            dq = dq + dot(p_ref[n, c], kv[g, rows(t, c), :], TN)
        head = pl.ds(pl.multiple_of((g * 4 + h) * DH, DH), DH)
        dq_s[pl.ds(pl.multiple_of(t * T, T), T), head] = (dq * FACTOR).astype(BF)
        return 0

    lax.fori_loop(0, 16, phase3, 0)
    for copy in dq_swap(1):
        copy.start()
    w_done()
    w_load.wait()
    for i in range(8):
        a, j = i // 4, i % 4
        rows_of = weight[a, j].reshape(512, 4 * DH)
        in_out[:, i * 512 : (i + 1) * 512] = dot(vd[...], rows_of, NT).astype(BF)
    give_total(3)
    w_end()
    for g in (0, 1):
        for copy in dq_swap(g) + spread(2 + g) + keep(2 + g):
            copy.wait()
    for u in range(4):
        for k in (1, 2, 3):
            give(u, k).wait_send()

        @pl.when(has_prev)
        def _():
            back(u).wait_send()

    for copy in x_along():
        copy.wait_send()
    for i in range(7):
        swaps[i].wait_send()
    sg_swap.wait_send()
    for u in range(5):

        @pl.when(has_next)
        def _():
            forth(u).wait_send()

        for k in (1, 2, 3):
            along(u, k, 4).wait_send()


def attend(q, do, o, k, v, sg, x, w):
    dma = pltpu.SemaphoreType.DMA
    vmem = pltpu.VMEM
    return pl.pallas_call(
        main_kernel,
        in_specs=[ANY] * 5 + [VM, ANY, ANY],
        out_specs=[VM, VM, VM, VM, ANY],
        out_shape=[
            jax.ShapeDtypeStruct((T, 16 * DH), BF),
            jax.ShapeDtypeStruct((T, 4 * DH), BF),
            jax.ShapeDtypeStruct((T, 4096), BF),
            jax.ShapeDtypeStruct((64, 4 * DH), F32),
            jax.ShapeDtypeStruct((2, 4, 4, 2, 64, 4 * DH), BF),
        ],
        scratch_shapes=[
            vmem((CHIP, 8 * DH), BF),
            vmem((CHIP, 8 * DH), BF),
            vmem((CHIP, 8 * DH), BF),
            vmem((4, WIN, DH), BF),
            vmem((5, 2, 8, T), jnp.int32),
            vmem((2, NK, T, T), F32),
            vmem((NK, T, T), F32),
            vmem((16, NK, T, T), BF),
            vmem((WIN, DH), F32),
            vmem((CHIP, 8 * DH), BF),
            vmem((4, WIN, DH), BF),
            vmem((4, 3, CHIP, DH), BF),
            vmem((4, CHIP, DH), BF),
            vmem((4, CHIP, DH), BF),
            vmem((4, 2, T, DH), BF),
            vmem((T, 4 * DH), BF),
            vmem((2, 4, T, 2 * DH), BF),
            vmem((2, 4, 2, T, 512), BF),
            vmem((2, 4, 128, 2 * DH), BF),
            vmem((3, 2, 128, 2 * DH), BF),
            vmem((2, 2, 64, 2 * DH), BF),
            vmem((2, 8, 64, 2 * DH), BF),
            vmem((2, 4, 4, 2, 64, 4 * DH), BF),
            dma((19,)), dma((14,)), dma((14,)), dma((5,)), dma((5,)), dma((5, 3)), dma((5, 3)),
            dma((4, 3)), dma((4, 3)), dma((4,)), dma((4,)),
            dma((2, 3)), dma((2, 3)), dma((3, 2)), dma((3, 2)), dma((4,)), dma((4,)),
            dma((3,)), dma((3,)), dma((2, 8)), dma((2, 8)), dma((9,)), dma((10,)),
        ],
        compiler_params=pltpu.CompilerParams(
            collective_id=0, has_side_effects=True, vmem_limit_bytes=60 << 20
        ),
        name="attend",
    )(q, do, o, k, v, sg, x, w)


def on_device(
    inputs, value_weight, query_states, key_states, value_states, attention_out, out_grad, segment_ids
):
    query_grad, key_grad, input_grad, weight_grad, _ = attend(
        query_states[0],
        out_grad[0],
        attention_out[0],
        key_states[0],
        value_states[0],
        segment_ids,
        inputs[0],
        value_weight,
    )
    return (query_grad[None], key_grad[None], input_grad[None], weight_grad)


def solution(mesh):
    placed = (
        P("dp", "ctx", None),
        P("ctx", None),
        P("dp", "ctx", None),
        P("dp", "ctx", None),
        P("dp", "ctx", None),
        P("dp", "ctx", None),
        P("dp", "ctx", None),
        P("dp", "ctx"),
    )
    return jax.shard_map(
        on_device,
        mesh=mesh,
        in_specs=placed,
        out_specs=(
            P("dp", "ctx", None),
            P("dp", "ctx", None),
            P("dp", "ctx", None),
            P("ctx", None),
        ),
        check_vma=False,
    )
```

```python
import math

import jax
import jax.numpy as jnp
from jax import lax
from jax.experimental import pallas as pl
from jax.experimental.pallas import tpu as pltpu
from jax.sharding import PartitionSpec as P

DH = 128
W = 2048
T = 256
CHIP = 2 * T
NK = W // T + 1
WIN = W + CHIP
FACTOR = 1.0 / math.sqrt(DH)
FACTOR2 = FACTOR * math.log2(math.e)
BF = jnp.bfloat16
F32 = jnp.float32
MESH = pl.DeviceIdType.MESH
ANY = pl.BlockSpec(memory_space=pl.ANY)
VM = pl.BlockSpec(memory_space=pltpu.VMEM)
NT = (((1,), (1,)), ((), ()))
NN = (((1,), (0,)), ((), ()))
TN = (((0,), (0,)), ((), ()))


def dot(a, b, dims):
    return lax.dot_general(a, b, dims, preferred_element_type=F32)


def signal(sem, ctx):
    pl.semaphore_signal(sem, inc=1, device_id={"ctx": ctx}, device_id_type=MESH)


def remote(src, dst, send, recv, ctx):
    return pltpu.make_async_remote_copy(
        src_ref=src,
        dst_ref=dst,
        send_sem=send,
        recv_sem=recv,
        device_id={"ctx": ctx},
        device_id_type=MESH,
    )


def main_kernel(
    q_in, do_in, o_in, k_in, v_in, sg_in, x_in, w_in,
    dq_out, dk_out, in_out, w_out,
    q_s, do_s, o_s, kv, sg, bias, s_ref, p_ref, acc, dq_s, gp, got, part, ahead, total,
    vd, vx, xg, wpart, wgot, wsum, far, weight,
    lsem, psend, precv, asend, arecv, rsend, rrecv, gsend, grecv, hsend, hrecv,
    vsend, vrecv, xsend, xrecv, fsend, frecv, ysend, yrecv, zsend, zrecv, wsend, wrecv,
):
    me = lax.axis_index("ctx")
    core = lax.rem(me, 2)
    other = 1 - core
    y = lax.rem(me // 2, 4)
    x = lax.rem(me // 8, 4)
    partner = me + 1 - 2 * core
    has_next = me < 56
    has_prev = me >= 8
    low = lax.axis_index("dp")
    high = me // 32
    place = lax.rem(me, 32)
    far_next = (x == 3) & has_next
    far_prev = (x == 0) & has_prev

    def row_peer(k):
        return me - 2 * y + 2 * lax.rem(y + k, 4)

    def column_peer(k):
        return me - 8 * x + 8 * lax.rem(x + k, 4)

    def z_peer(j, c):
        to = lax.rem(high * 4 + low + j, 8)
        return {"dp": lax.rem(to, 4), "ctx": (to // 4) * 32 + place - core + c}, to // 4

    barrier = pltpu.get_barrier_semaphore()
    for j in range(8):
        for c in (core, other):
            if j or c is other:
                pl.semaphore_signal(
                    barrier, inc=1, device_id=z_peer(j, c)[0], device_id_type=MESH
                )
    for k in (1, 2, 3):
        signal(barrier, row_peer(k))
        signal(barrier, column_peer(k))

    @pl.when(far_next)
    def _():
        signal(barrier, me + 8)

    @pl.when(far_prev)
    def _():
        signal(barrier, me - 8)

    sg[4, core] = jnp.broadcast_to(sg_in[...], (8, T))

    @pl.when(jnp.logical_not(has_prev))
    def _():
        kv[:, :CHIP, :] = jnp.zeros((4, CHIP, DH), BF)
        sg[0] = jnp.full((2, 8, T), -1, jnp.int32)

    pl.semaphore_wait(barrier, 21 + far_next.astype(jnp.int32) + far_prev.astype(jnp.int32))

    half = pl.ds(pl.multiple_of(core * T, T), T)
    rest = pl.ds(pl.multiple_of(other * T, T), T)
    home = pl.ds(pl.multiple_of(W + core * T, T), T)

    def cols(start, n):
        return pl.ds(pl.multiple_of(start * n, n), n)

    def source(i, c):
        if i < 4:
            return (k_in, v_in)[i // 2].at[:, cols(c * 2 + i % 2, DH)]
        return (q_in, do_in, o_in)[i - 4].at[:, cols(c, 8 * DH)]

    def target(i):
        if i < 4:
            return kv.at[i, home, :]
        return (q_s, do_s, o_s)[i - 4].at[half, :]

    swaps = [remote(source(i, other), target(i), psend.at[i], precv.at[i], partner) for i in range(7)]
    stays = [pltpu.make_async_copy(source(i, core), target(i), lsem.at[i]) for i in range(7)]
    sg_swap = remote(sg.at[4, core], sg.at[4, core], psend.at[7], precv.at[7], partner)

    def both(i):
        stays[i].start()
        swaps[i].start()

    both(0)
    sg_swap.start()
    both(4)
    both(5)

    def block(u, s):
        if u == 4:
            return sg.at[s]
        return kv.at[u, pl.ds(s * CHIP, CHIP), :]

    def forth(u):
        return remote(block(u, 4), block(u, 0), asend.at[u], arecv.at[u], me + 8)

    def along(u, k, s):
        return remote(
            block(u, s), block(u, 4 - k), rsend.at[u, k - 1], rrecv.at[u, k - 1], row_peer(k)
        )

    def send_ahead(u):
        if u == 4:
            sg_swap.wait_recv()
        else:
            stays[u].wait()
            swaps[u].wait_recv()

        @pl.when(has_next)
        def _():
            forth(u).start()

    def send_own(u):
        for k in (1, 2, 3):

            @pl.when(y + k < 4)
            def _():
                along(u, k, 4).start()

    def relay(u):
        @pl.when(has_prev)
        def _():
            forth(u).wait_recv()

        for k in (1, 2, 3):

            @pl.when(y + k >= 4)
            def _():
                along(u, k, 0).start()

    def arrived(u):
        for k in (1, 2, 3):
            along(u, k, 4).wait_recv()

    send_ahead(4)
    send_own(4)
    send_ahead(0)
    send_own(0)
    for i in (1, 2, 3, 6):
        both(i)
    relay(4)
    relay(0)
    for i in (4, 5):
        stays[i].wait()
        swaps[i].wait_recv()
    arrived(4)

    for i in range(NK + 1):
        sk = jnp.transpose(sg[i // 2, i % 2].astype(F32))[:, :1]
        sk = jnp.broadcast_to(sk, (T, T))
        for t in (0, 1):
            c = i - t
            if 0 <= c < NK:
                live = sk == sg[4, t][:1, :].astype(F32)
                kpos = lax.broadcasted_iota(jnp.int32, (T, T), 0)
                qpos = lax.broadcasted_iota(jnp.int32, (T, T), 1)
                if c == 0:
                    live = live & (kpos > qpos)
                if c == NK - 1:
                    live = live & (kpos <= qpos)
                bias[t, c] = jnp.where(live, 0.0, -1e30)
    arrived(0)

    zed = high * 4 + low

    def w_at(x_at, y_at, z, c):
        return weight.at[z // 4, x_at, y_at, c, :, cols(lax.rem(z, 4), DH)]

    every = slice(None)
    w_mine = w_in.at[:, cols(low, DH)]
    w_stay = pltpu.make_async_copy(w_mine, w_at(x, y, zed, core), lsem.at[17])

    def w_x(k):
        return remote(
            w_mine, w_at(x, y, zed, core), wsend.at[k - 1], wrecv.at[k - 1], column_peer(k)
        )

    def w_y(k):
        block = w_at(every, y, zed, core)
        return remote(block, block, wsend.at[2 + k], wrecv.at[2 + k], row_peer(k))

    def w_up(i):
        block = w_at(every, every, lax.rem(zed + 8 - i, 8), core)
        return w_round(block, wsend.at[6 + i], wrecv.at[6 + i], 1)

    def w_down(i):
        block = w_at(every, every, lax.rem(zed + i, 8), core)
        return w_round(block, wsend.at[10 + i], wrecv.at[10 + i], 7)

    def w_round(block, send, recv, j):
        return pltpu.make_async_remote_copy(
            src_ref=block,
            dst_ref=block,
            send_sem=send,
            recv_sem=recv,
            device_id=z_peer(j, core)[0],
            device_id_type=MESH,
        )

    w_half = weight.at[:, :, :, core]
    w_hand = remote(w_half, w_half, wsend.at[13], wrecv.at[13], partner)

    def w_begin():
        w_stay.start()
        for k in (1, 2, 3):
            w_x(k).start()

    def w_along_y():
        w_stay.wait()
        for k in (1, 2, 3):
            w_x(k).wait_recv()
        for k in (1, 2, 3):
            w_y(k).start()

    def w_turn(i):
        if i == 0:
            for k in (1, 2, 3):
                w_y(k).wait_recv()
        else:
            w_up(i - 1).wait_recv()
            if i < 4:
                w_down(i - 1).wait_recv()
        w_up(i).start()
        if i < 3:
            w_down(i).start()

    def w_across():
        w_up(3).wait_recv()
        w_hand.start()

    def w_done():
        w_hand.wait()
        for k in (1, 2, 3):
            w_x(k).wait_send()
            w_y(k).wait_send()
        for i in range(4):
            w_up(i).wait_send()
        for i in range(3):
            w_down(i).wait_send()

    def give(g, k):
        return remote(
            gp.at[g, pl.ds((4 - k) * CHIP, CHIP), :],
            got.at[g, k - 1],
            gsend.at[g, k - 1],
            grecv.at[g, k - 1],
            row_peer(4 - k),
        )

    def back(g):
        return remote(part.at[g], ahead.at[g], hsend.at[g], hrecv.at[g], me - 8)

    def give_start(g):
        for k in (1, 2, 3):
            give(g, k).start()

    def give_sum(g):
        for k in (1, 2, 3):
            give(g, k).wait_recv()
        before = gp[g, :CHIP, :].astype(F32)
        for k in (1, 2, 3):
            before = before + jnp.where(y + k >= 4, got[g, k - 1].astype(F32), 0.0)
        part[g] = before.astype(BF)

        @pl.when(has_prev)
        def _():
            back(g).start()

    def spread(u):
        g = u % 2
        columns = cols(core * 2 + g, DH)
        dst = vd if u < 2 else dk_out
        copies = [
            remote(total.at[u, other], dst.at[:, columns], psend.at[8 + u], precv.at[8 + u], partner)
        ]
        if u < 2:
            copies += [
                remote(
                    total.at[u],
                    vx.at[:, k, :, pl.ds(g * DH, DH)],
                    vsend.at[g, k - 1],
                    vrecv.at[g, k - 1],
                    column_peer(k),
                )
                for k in (1, 2, 3)
            ]
        return copies

    def keep(u):
        g = u % 2
        columns = cols(core * 2 + g, DH)
        if u < 2:
            return [
                pltpu.make_async_copy(total.at[u, core], vd.at[:, columns], lsem.at[8 + u]),
                pltpu.make_async_copy(total.at[u], vx.at[:, 0, :, pl.ds(g * DH, DH)], lsem.at[10 + u]),
            ]
        return [pltpu.make_async_copy(total.at[u, core], dk_out.at[:, columns], lsem.at[8 + u])]

    def give_total(g):
        @pl.when(has_next)
        def _():
            back(g).wait_recv()

        @pl.when(jnp.logical_not(has_next))
        def _():
            ahead[g] = jnp.zeros((CHIP, DH), BF)

        mine = gp[g, W:, :].astype(F32) + ahead[g].astype(F32)
        for k in (1, 2, 3):
            mine = mine + jnp.where(y + k < 4, got[g, k - 1].astype(F32), 0.0)
        total[g] = mine.astype(BF).reshape(2, T, DH)
        for copy in spread(g) + keep(g):
            copy.start()

    def strip(k, high):
        start = pl.multiple_of(high * 2048 + lax.rem(x + k, 4) * 512, 512)
        return x_in.at[:, pl.ds(start, 512)]

    def x_keep():
        return [pltpu.make_async_copy(strip(0, i), xg.at[core, 0, i], lsem.at[12 + i]) for i in (0, 1)]

    def x_along(ks=(1, 2, 3)):
        return [
            remote(
                strip(k, i), xg.at[core, k, i], xsend.at[k - 1, i], xrecv.at[k - 1, i], column_peer(k)
            )
            for k in ks
            for i in (0, 1)
        ]

    def x_forward(ks=(0, 1, 2, 3)):
        return [
            remote(xg.at[core, k], xg.at[core, k], fsend.at[k], frecv.at[k], partner) for k in ks
        ]

    def at(n, when, *calls):
        @pl.when(n == when)
        def _():
            for f, *args in calls:
                f(*args)

    def start_all(make):
        for copy in make():
            copy.start()

    def x_pass(*ks):
        for copy in x_along(ks) if ks[0] else x_keep():
            copy.wait_recv() if ks[0] else copy.wait()
        for copy in x_forward(ks):
            copy.start()

    def w_part(g):
        if g == 0:
            for copy in x_forward():
                copy.wait()
        for copy in spread(g) + keep(g):
            copy.wait()
        for i in (0, 1):
            sums = jnp.zeros((512, DH), F32)
            for a in (0, 1):
                for k in range(4):
                    sums = sums + dot(xg[a, k, i], vx[a, k, :, g * DH : (g + 1) * DH], TN)
            wpart[g, i] = sums.astype(BF).reshape(4, 128, DH)
        for copy in y_sends(g):
            copy.start()

    def y_sends(g):
        return [
            remote(
                wpart.at[g, :, lax.rem(y + k, 4)],
                wgot.at[g, k - 1],
                ysend.at[g, k - 1],
                yrecv.at[g, k - 1],
                row_peer(k),
            )
            for k in (1, 2, 3)
        ]

    def z_sends(g):
        copies = []
        for j in range(8):
            for i in (0, 1):
                peer, part_of = z_peer(j, core if i == 0 else other)
                src = wsum.at[g, part_of, core if i == 0 else other]
                if j == 0 and i == 0:
                    copies.append(pltpu.make_async_copy(src, far.at[g, 0, 0], lsem.at[18 + g]))
                else:
                    copies.append(
                        pltpu.make_async_remote_copy(
                            src_ref=src,
                            dst_ref=far.at[g, i, j],
                            send_sem=zsend.at[g, i, j],
                            recv_sem=zrecv.at[g, i, j],
                            device_id=peer,
                            device_id_type=MESH,
                        )
                    )
        return copies

    def w_sum(g):
        for copy in y_sends(g):
            copy.wait_recv()
        sums = wpart[g, :, y].astype(F32)
        for k in range(3):
            sums = sums + wgot[g, k].astype(F32)
        wsum[g] = sums.astype(BF).reshape(2, 2, 64, DH)
        for copy in z_sends(g):
            copy.start()

    def w_end(g):
        for copy in z_sends(g):
            copy.wait()
        for copy in y_sends(g):
            copy.wait_send()
        for i in (0, 1):
            sums = far[g, i, 0].astype(F32)
            for j in range(1, 8):
                sums = sums + far[g, i, j].astype(F32)
            w_out[:, cols((core if i == 0 else other) * 2 + g, DH)] = sums

    def rows(t, c):
        return pl.ds(pl.multiple_of(t * T + c * T, T), T)

    def phase1(n, _):
        g, h, t = n // 8, lax.rem(n // 2, 4), lax.rem(n, 2)
        at(n, 0, (send_ahead, 1), (send_own, 1), (send_ahead, 2), (send_ahead, 3), (w_begin,))
        at(n, 1, (start_all, x_keep), (start_all, lambda: x_along((3,))))
        at(n, 2, (w_along_y,))
        at(n, 3, (relay, 1), (send_own, 2), (x_pass, 0))
        at(n, 5, (start_all, lambda: x_along((1,))))
        at(n, 6, (relay, 2), (send_own, 3))
        at(n, 7, (w_turn, 0), (start_all, lambda: x_along((2,))))
        at(n, 8, (arrived, 1))
        at(n, 9, (give_start, 0), (relay, 3))
        at(n, 12, (w_turn, 1), (x_pass, 3))

        @pl.when(lax.rem(n, 8) == 0)
        def _():
            acc[...] = jnp.zeros_like(acc)

        head = pl.ds(pl.multiple_of((g * 4 + h) * DH, DH), DH)
        here = pl.ds(pl.multiple_of(t * T, T), T)
        q, do = q_s[here, head], do_s[here, head]
        top = jnp.full((8, T), -1e30, F32)
        for c in range(NK):
            s = dot(kv[g, rows(t, c), :], q, NT) + bias[t, c]
            s_ref[c] = s
            top = jnp.maximum(top, jnp.max(s.reshape(T // 8, 8, T), axis=0))
        top = jnp.max(top, axis=0, keepdims=True)
        weight = jnp.zeros((8, T), F32)
        for c in range(NK):
            e = jnp.exp2((s_ref[c] - top) * FACTOR2)
            s_ref[c] = e
            weight = weight + jnp.sum(e.reshape(T // 8, 8, T), axis=0)
        inverse = 1.0 / jnp.sum(weight, axis=0, keepdims=True)
        for c in range(NK):
            p = (s_ref[c] * inverse).astype(BF)
            p_ref[n, c] = p
            acc[rows(t, c), :] += dot(p, do, NN)

        @pl.when(lax.rem(n, 8) == 7)
        def _():
            gp[g] = acc[...].astype(BF)

        return 0

    lax.fori_loop(0, 16, phase1, 0)

    def dq_swap(g):
        block = pl.ds(g * 4 * DH, 4 * DH)
        place = cols(core * 2 + g, 4 * DH)
        return [
            remote(dq_s.at[rest, block], dq_out.at[:, place], psend.at[12 + g], precv.at[12 + g], partner),
            pltpu.make_async_copy(dq_s.at[half, block], dq_out.at[:, place], lsem.at[14 + g]),
        ]

    stays[6].wait()
    swaps[6].wait_recv()
    give_start(1)
    arrived(2)

    def phase2(n, _):
        g, h, t = n // 8, lax.rem(n // 2, 4), lax.rem(n, 2)
        at(n, 1, (give_sum, 0))
        at(n, 2, (w_turn, 2))
        at(n, 5, (give_total, 0))
        at(n, 7, (give_sum, 1))
        at(n, 8, (arrived, 3), (give_start, 2), (x_pass, 1, 2))
        at(n, 9, (w_turn, 3))
        at(n, 12, (give_total, 1))
        at(n, 14, (w_part, 0))
        at(n, 15, (give_sum, 2))

        @pl.when(lax.rem(n, 8) == 0)
        def _():
            acc[...] = jnp.zeros_like(acc)

        head = pl.ds(pl.multiple_of((g * 4 + h) * DH, DH), DH)
        here = pl.ds(pl.multiple_of(t * T, T), T)
        q, do = q_s[here, head], do_s[here, head]
        product = do.astype(F32) * o_s[here, head].astype(F32)
        delta = jnp.sum(jnp.transpose(product), axis=0, keepdims=True)
        for c in range(NK):
            dp = dot(kv[2 + g, rows(t, c), :], do, NT)
            ds = (p_ref[n, c].astype(F32) * (dp - delta)).astype(BF)
            p_ref[n, c] = ds
            acc[rows(t, c), :] += dot(ds, q, NN)

        @pl.when(lax.rem(n, 8) == 7)
        def _():
            gp[2 + g] = (acc[...] * FACTOR).astype(BF)

        return 0

    lax.fori_loop(0, 16, phase2, 0)
    give_start(3)
    w_across()

    def phase3(n, _):
        g, h, t = n // 8, lax.rem(n // 2, 4), lax.rem(n, 2)
        at(n, 3, (w_sum, 0), (w_part, 1))
        at(n, 8, (give_total, 2), (start_all, lambda: dq_swap(0)))
        at(n, 12, (w_sum, 1))
        at(n, 14, (give_sum, 3))
        dq = jnp.zeros((T, DH), F32)
        for c in range(NK):
            dq = dq + dot(p_ref[n, c], kv[g, rows(t, c), :], TN)
        head = pl.ds(pl.multiple_of((g * 4 + h) * DH, DH), DH)
        dq_s[pl.ds(pl.multiple_of(t * T, T), T), head] = (dq * FACTOR).astype(BF)
        return 0

    lax.fori_loop(0, 16, phase3, 0)
    for copy in dq_swap(1):
        copy.start()
    w_done()
    for i in range(8):
        a, j = i // 4, i % 4
        rows_of = weight[a, j].reshape(512, 4 * DH)
        in_out[:, i * 512 : (i + 1) * 512] = dot(vd[...], rows_of, NT).astype(BF)
    give_total(3)
    w_end(0)
    w_end(1)
    for g in (0, 1):
        for copy in dq_swap(g) + spread(2 + g) + keep(2 + g):
            copy.wait()
    for u in range(4):
        for k in (1, 2, 3):
            give(u, k).wait_send()

        @pl.when(has_prev)
        def _():
            back(u).wait_send()

    for copy in x_along():
        copy.wait_send()
    for i in range(7):
        swaps[i].wait_send()
    sg_swap.wait_send()
    for u in range(5):

        @pl.when(has_next)
        def _():
            forth(u).wait_send()

        for k in (1, 2, 3):
            along(u, k, 4).wait_send()


def attend(q, do, o, k, v, sg, x, w):
    dma = pltpu.SemaphoreType.DMA
    vmem = pltpu.VMEM
    return pl.pallas_call(
        main_kernel,
        in_specs=[ANY] * 5 + [VM, ANY, ANY],
        out_specs=[VM] * 4,
        out_shape=[
            jax.ShapeDtypeStruct((T, 16 * DH), BF),
            jax.ShapeDtypeStruct((T, 4 * DH), BF),
            jax.ShapeDtypeStruct((T, 4096), BF),
            jax.ShapeDtypeStruct((64, 4 * DH), F32),
        ],
        scratch_shapes=[
            vmem((CHIP, 8 * DH), BF),
            vmem((CHIP, 8 * DH), BF),
            vmem((CHIP, 8 * DH), BF),
            vmem((4, WIN, DH), BF),
            vmem((5, 2, 8, T), jnp.int32),
            vmem((2, NK, T, T), F32),
            vmem((NK, T, T), F32),
            vmem((16, NK, T, T), BF),
            vmem((WIN, DH), F32),
            vmem((CHIP, 8 * DH), BF),
            vmem((4, WIN, DH), BF),
            vmem((4, 3, CHIP, DH), BF),
            vmem((4, CHIP, DH), BF),
            vmem((4, CHIP, DH), BF),
            vmem((4, 2, T, DH), BF),
            vmem((T, 4 * DH), BF),
            vmem((2, 4, T, 2 * DH), BF),
            vmem((2, 4, 2, T, 512), BF),
            vmem((2, 2, 4, 128, DH), BF),
            vmem((2, 3, 2, 128, DH), BF),
            vmem((2, 2, 2, 64, DH), BF),
            vmem((2, 2, 8, 64, DH), BF),
            vmem((2, 4, 4, 2, 64, 4 * DH), BF),
            dma((20,)), dma((14,)), dma((14,)), dma((5,)), dma((5,)), dma((5, 3)), dma((5, 3)),
            dma((4, 3)), dma((4, 3)), dma((4,)), dma((4,)),
            dma((2, 3)), dma((2, 3)), dma((3, 2)), dma((3, 2)), dma((4,)), dma((4,)),
            dma((2, 3)), dma((2, 3)), dma((2, 2, 8)), dma((2, 2, 8)), dma((14,)), dma((14,)),
        ],
        compiler_params=pltpu.CompilerParams(
            collective_id=0, has_side_effects=True, vmem_limit_bytes=60 << 20
        ),
        name="attend",
    )(q, do, o, k, v, sg, x, w)


def on_device(
    inputs, value_weight, query_states, key_states, value_states, attention_out, out_grad, segment_ids
):
    query_grad, key_grad, input_grad, weight_grad = attend(
        query_states[0],
        out_grad[0],
        attention_out[0],
        key_states[0],
        value_states[0],
        segment_ids,
        inputs[0],
        value_weight,
    )
    return (query_grad[None], key_grad[None], input_grad[None], weight_grad)


def solution(mesh):
    placed = (
        P("dp", "ctx", None),
        P("ctx", None),
        P("dp", "ctx", None),
        P("dp", "ctx", None),
        P("dp", "ctx", None),
        P("dp", "ctx", None),
        P("dp", "ctx", None),
        P("dp", "ctx"),
    )
    return jax.shard_map(
        on_device,
        mesh=mesh,
        in_specs=placed,
        out_specs=(
            P("dp", "ctx", None),
            P("dp", "ctx", None),
            P("dp", "ctx", None),
            P("ctx", None),
        ),
        check_vma=False,
    )
```

```python
import math

import jax
import jax.numpy as jnp
from jax import lax
from jax.experimental import pallas as pl
from jax.experimental.pallas import tpu as pltpu
from jax.sharding import PartitionSpec as P

DH = 128
W = 2048
T = 256
CHIP = 2 * T
NK = W // T + 1
WIN = W + CHIP
FACTOR = 1.0 / math.sqrt(DH)
FACTOR2 = FACTOR * math.log2(math.e)
BF = jnp.bfloat16
F32 = jnp.float32
MESH = pl.DeviceIdType.MESH
ANY = pl.BlockSpec(memory_space=pl.ANY)
VM = pl.BlockSpec(memory_space=pltpu.VMEM)
NT = (((1,), (1,)), ((), ()))
NN = (((1,), (0,)), ((), ()))
TN = (((0,), (0,)), ((), ()))


def dot(a, b, dims):
    return lax.dot_general(a, b, dims, preferred_element_type=F32)


def signal(sem, ctx):
    pl.semaphore_signal(sem, inc=1, device_id={"ctx": ctx}, device_id_type=MESH)


def remote(src, dst, send, recv, ctx):
    return pltpu.make_async_remote_copy(
        src_ref=src,
        dst_ref=dst,
        send_sem=send,
        recv_sem=recv,
        device_id={"ctx": ctx},
        device_id_type=MESH,
    )


def main_kernel(
    q_in, do_in, o_in, k_in, v_in, sg_in, x_in, w_in,
    dq_out, dk_out, in_out, w_out,
    q_s, do_s, o_s, kv, sg, bias, s_ref, p_ref, acc, dq_s, gp, got, part, ahead, total,
    vd, vx, xg, wpart, wgot, wsum, far, weight,
    lsem, psend, precv, asend, arecv, rsend, rrecv, gsend, grecv, hsend, hrecv,
    vsend, vrecv, xsend, xrecv, fsend, frecv, ysend, yrecv, zsend, zrecv, wsend, wrecv,
):
    me = lax.axis_index("ctx")
    core = lax.rem(me, 2)
    other = 1 - core
    y = lax.rem(me // 2, 4)
    x = lax.rem(me // 8, 4)
    partner = me + 1 - 2 * core
    has_next = me < 56
    has_prev = me >= 8
    low = lax.axis_index("dp")
    high = me // 32
    place = lax.rem(me, 32)
    far_next = (x == 3) & has_next
    far_prev = (x == 0) & has_prev

    def row_peer(k):
        return me - 2 * y + 2 * lax.rem(y + k, 4)

    def column_peer(k):
        return me - 8 * x + 8 * lax.rem(x + k, 4)

    def z_peer(j, c):
        to = lax.rem(high * 4 + low + j, 8)
        return {"dp": lax.rem(to, 4), "ctx": (to // 4) * 32 + place - core + c}, to // 4

    barrier = pltpu.get_barrier_semaphore()
    for j in range(8):
        for c in (core, other):
            if j or c is other:
                pl.semaphore_signal(
                    barrier, inc=1, device_id=z_peer(j, c)[0], device_id_type=MESH
                )
    for k in (1, 2, 3):
        signal(barrier, row_peer(k))
        signal(barrier, column_peer(k))

    @pl.when(far_next)
    def _():
        signal(barrier, me + 8)

    @pl.when(far_prev)
    def _():
        signal(barrier, me - 8)

    sg[4, core] = jnp.broadcast_to(sg_in[...], (8, T))

    @pl.when(jnp.logical_not(has_prev))
    def _():
        kv[:, :CHIP, :] = jnp.zeros((4, CHIP, DH), BF)
        sg[0] = jnp.full((2, 8, T), -1, jnp.int32)

    pl.semaphore_wait(barrier, 21 + far_next.astype(jnp.int32) + far_prev.astype(jnp.int32))

    half = pl.ds(pl.multiple_of(core * T, T), T)
    rest = pl.ds(pl.multiple_of(other * T, T), T)
    home = pl.ds(pl.multiple_of(W + core * T, T), T)

    def cols(start, n):
        return pl.ds(pl.multiple_of(start * n, n), n)

    def source(i, c):
        if i < 4:
            return (k_in, v_in)[i // 2].at[:, cols(c * 2 + i % 2, DH)]
        return (q_in, do_in, o_in)[i - 4].at[:, cols(c, 8 * DH)]

    def target(i):
        if i < 4:
            return kv.at[i, home, :]
        return (q_s, do_s, o_s)[i - 4].at[half, :]

    swaps = [remote(source(i, other), target(i), psend.at[i], precv.at[i], partner) for i in range(7)]
    stays = [pltpu.make_async_copy(source(i, core), target(i), lsem.at[i]) for i in range(7)]
    sg_swap = remote(sg.at[4, core], sg.at[4, core], psend.at[7], precv.at[7], partner)

    def both(i):
        stays[i].start()
        swaps[i].start()

    both(0)
    sg_swap.start()
    both(4)
    both(5)

    def block(u, s):
        if u == 4:
            return sg.at[s]
        return kv.at[u, pl.ds(s * CHIP, CHIP), :]

    def forth(u):
        return remote(block(u, 4), block(u, 0), asend.at[u], arecv.at[u], me + 8)

    def along(u, k, s):
        return remote(
            block(u, s), block(u, 4 - k), rsend.at[u, k - 1], rrecv.at[u, k - 1], row_peer(k)
        )

    def send_ahead(u):
        if u == 4:
            sg_swap.wait_recv()
        else:
            stays[u].wait()
            swaps[u].wait_recv()

        @pl.when(has_next)
        def _():
            forth(u).start()

    def send_own(u):
        for k in (1, 2, 3):

            @pl.when(y + k < 4)
            def _():
                along(u, k, 4).start()

    def relay(u):
        @pl.when(has_prev)
        def _():
            forth(u).wait_recv()

        for k in (1, 2, 3):

            @pl.when(y + k >= 4)
            def _():
                along(u, k, 0).start()

    def arrived(u):
        for k in (1, 2, 3):
            along(u, k, 4).wait_recv()

    send_ahead(4)
    send_own(4)
    send_ahead(0)
    send_own(0)
    for i in (1, 2, 3, 6):
        both(i)
    relay(4)
    relay(0)
    for i in (4, 5):
        stays[i].wait()
        swaps[i].wait_recv()
    arrived(4)

    for i in range(NK + 1):
        sk = jnp.transpose(sg[i // 2, i % 2].astype(F32))[:, :1]
        sk = jnp.broadcast_to(sk, (T, T))
        for t in (0, 1):
            c = i - t
            if 0 <= c < NK:
                live = sk == sg[4, t][:1, :].astype(F32)
                kpos = lax.broadcasted_iota(jnp.int32, (T, T), 0)
                qpos = lax.broadcasted_iota(jnp.int32, (T, T), 1)
                if c == 0:
                    live = live & (kpos > qpos)
                if c == NK - 1:
                    live = live & (kpos <= qpos)
                bias[t, c] = jnp.where(live, 0.0, -1e30)
    arrived(0)

    zed = high * 4 + low

    def w_at(x_at, y_at, z, c):
        return weight.at[z // 4, x_at, y_at, c, :, cols(lax.rem(z, 4), DH)]

    every = slice(None)
    w_mine = w_in.at[:, cols(low, DH)]
    w_stay = pltpu.make_async_copy(w_mine, w_at(x, y, zed, core), lsem.at[17])

    def w_x(k):
        return remote(
            w_mine, w_at(x, y, zed, core), wsend.at[k - 1], wrecv.at[k - 1], column_peer(k)
        )

    def w_y(k):
        block = w_at(every, y, zed, core)
        return remote(block, block, wsend.at[2 + k], wrecv.at[2 + k], row_peer(k))

    def w_up(i):
        block = w_at(every, every, lax.rem(zed + 8 - i, 8), core)
        return w_round(block, wsend.at[6 + i], wrecv.at[6 + i], 1)

    def w_down(i):
        block = w_at(every, every, lax.rem(zed + i, 8), core)
        return w_round(block, wsend.at[10 + i], wrecv.at[10 + i], 7)

    def w_round(block, send, recv, j):
        return pltpu.make_async_remote_copy(
            src_ref=block,
            dst_ref=block,
            send_sem=send,
            recv_sem=recv,
            device_id=z_peer(j, core)[0],
            device_id_type=MESH,
        )

    w_half = weight.at[:, :, :, core]
    w_hand = remote(w_half, w_half, wsend.at[13], wrecv.at[13], partner)

    def w_begin():
        w_stay.start()
        for k in (1, 2, 3):
            w_x(k).start()

    def w_along_y():
        w_stay.wait()
        for k in (1, 2, 3):
            w_x(k).wait_recv()
        for k in (1, 2, 3):
            w_y(k).start()

    def w_turn(i):
        if i == 0:
            for k in (1, 2, 3):
                w_y(k).wait_recv()
        else:
            w_up(i - 1).wait_recv()
            if i < 4:
                w_down(i - 1).wait_recv()
        w_up(i).start()
        if i < 3:
            w_down(i).start()

    def w_across():
        w_up(3).wait_recv()
        w_hand.start()

    def w_done():
        w_hand.wait()
        for k in (1, 2, 3):
            w_x(k).wait_send()
            w_y(k).wait_send()
        for i in range(4):
            w_up(i).wait_send()
        for i in range(3):
            w_down(i).wait_send()

    def give(g, k):
        return remote(
            gp.at[g, pl.ds((4 - k) * CHIP, CHIP), :],
            got.at[g, k - 1],
            gsend.at[g, k - 1],
            grecv.at[g, k - 1],
            row_peer(4 - k),
        )

    def back(g):
        return remote(part.at[g], ahead.at[g], hsend.at[g], hrecv.at[g], me - 8)

    def give_start(g):
        for k in (1, 2, 3):
            give(g, k).start()

    def give_sum(g):
        for k in (1, 2, 3):
            give(g, k).wait_recv()
        before = gp[g, :CHIP, :].astype(F32)
        for k in (1, 2, 3):
            before = before + jnp.where(y + k >= 4, got[g, k - 1].astype(F32), 0.0)
        part[g] = before.astype(BF)

        @pl.when(has_prev)
        def _():
            back(g).start()

    def spread(u):
        g = u % 2
        columns = cols(core * 2 + g, DH)
        dst = vd if u < 2 else dk_out
        copies = [
            remote(total.at[u, other], dst.at[:, columns], psend.at[8 + u], precv.at[8 + u], partner)
        ]
        if u < 2:
            copies += [
                remote(
                    total.at[u],
                    vx.at[:, k, :, pl.ds(g * DH, DH)],
                    vsend.at[g, k - 1],
                    vrecv.at[g, k - 1],
                    column_peer(k),
                )
                for k in (1, 2, 3)
            ]
        return copies

    def keep(u):
        g = u % 2
        columns = cols(core * 2 + g, DH)
        if u < 2:
            return [
                pltpu.make_async_copy(total.at[u, core], vd.at[:, columns], lsem.at[8 + u]),
                pltpu.make_async_copy(total.at[u], vx.at[:, 0, :, pl.ds(g * DH, DH)], lsem.at[10 + u]),
            ]
        return [pltpu.make_async_copy(total.at[u, core], dk_out.at[:, columns], lsem.at[8 + u])]

    def give_total(g):
        @pl.when(has_next)
        def _():
            back(g).wait_recv()

        @pl.when(jnp.logical_not(has_next))
        def _():
            ahead[g] = jnp.zeros((CHIP, DH), BF)

        mine = gp[g, W:, :].astype(F32) + ahead[g].astype(F32)
        for k in (1, 2, 3):
            mine = mine + jnp.where(y + k < 4, got[g, k - 1].astype(F32), 0.0)
        total[g] = mine.astype(BF).reshape(2, T, DH)
        for copy in spread(g) + keep(g):
            copy.start()

    def strip(k, high):
        start = pl.multiple_of(high * 2048 + lax.rem(x + k, 4) * 512, 512)
        return x_in.at[:, pl.ds(start, 512)]

    def x_keep():
        return [pltpu.make_async_copy(strip(0, i), xg.at[core, 0, i], lsem.at[12 + i]) for i in (0, 1)]

    def x_along(ks=(1, 2, 3)):
        return [
            remote(
                strip(k, i), xg.at[core, k, i], xsend.at[k - 1, i], xrecv.at[k - 1, i], column_peer(k)
            )
            for k in ks
            for i in (0, 1)
        ]

    def x_forward(ks=(0, 1, 2, 3)):
        return [
            remote(xg.at[core, k], xg.at[core, k], fsend.at[k], frecv.at[k], partner) for k in ks
        ]

    def at(n, when, *calls):
        @pl.when(n == when)
        def _():
            for f, *args in calls:
                f(*args)

    def start_all(make):
        for copy in make():
            copy.start()

    def x_pass(*ks):
        for copy in x_along(ks) if ks[0] else x_keep():
            copy.wait_recv() if ks[0] else copy.wait()
        for copy in x_forward(ks):
            copy.start()

    def w_part(g):
        if g == 0:
            for copy in x_forward():
                copy.wait()
        for copy in spread(g) + keep(g):
            copy.wait()
        for i in (0, 1):
            sums = jnp.zeros((512, DH), F32)
            for a in (0, 1):
                for k in range(4):
                    sums = sums + dot(xg[a, k, i], vx[a, k, :, g * DH : (g + 1) * DH], TN)
            wpart[g, i] = sums.astype(BF).reshape(4, 128, DH)
        for copy in y_sends(g):
            copy.start()

    def y_sends(g):
        return [
            remote(
                wpart.at[g, :, lax.rem(y + k, 4)],
                wgot.at[g, k - 1],
                ysend.at[g, k - 1],
                yrecv.at[g, k - 1],
                row_peer(k),
            )
            for k in (1, 2, 3)
        ]

    def z_sends(g):
        copies = []
        for j in range(8):
            for i in (0, 1):
                peer, part_of = z_peer(j, core if i == 0 else other)
                src = wsum.at[g, part_of, core if i == 0 else other]
                if j == 0 and i == 0:
                    copies.append(pltpu.make_async_copy(src, far.at[g, 0, 0], lsem.at[18 + g]))
                else:
                    copies.append(
                        pltpu.make_async_remote_copy(
                            src_ref=src,
                            dst_ref=far.at[g, i, j],
                            send_sem=zsend.at[g, i, j],
                            recv_sem=zrecv.at[g, i, j],
                            device_id=peer,
                            device_id_type=MESH,
                        )
                    )
        return copies

    def w_sum(g):
        for copy in y_sends(g):
            copy.wait_recv()
        sums = wpart[g, :, y].astype(F32)
        for k in range(3):
            sums = sums + wgot[g, k].astype(F32)
        wsum[g] = sums.astype(BF).reshape(2, 2, 64, DH)
        for copy in z_sends(g):
            copy.start()

    def w_end(g):
        for copy in z_sends(g):
            copy.wait()
        for copy in y_sends(g):
            copy.wait_send()
        for i in (0, 1):
            sums = far[g, i, 0].astype(F32)
            for j in range(1, 8):
                sums = sums + far[g, i, j].astype(F32)
            w_out[:, cols((core if i == 0 else other) * 2 + g, DH)] = sums

    def rows(t, c):
        return pl.ds(pl.multiple_of(t * T + c * T, T), T)

    def phase1(n, _):
        g, h, t = n // 8, lax.rem(n // 2, 4), lax.rem(n, 2)
        at(n, 0, (send_ahead, 1), (send_own, 1), (w_begin,))
        at(n, 1, (start_all, x_keep), (start_all, lambda: x_along((3,))))
        at(n, 2, (send_ahead, 2), (w_along_y,))
        at(n, 3, (relay, 1), (send_own, 2), (x_pass, 0))
        at(n, 4, (send_ahead, 3))
        at(n, 6, (w_turn, 0), (start_all, lambda: x_along((1,))))
        at(n, 8, (arrived, 1), (relay, 2), (send_own, 3), (start_all, lambda: x_along((2,))))
        at(n, 9, (give_start, 0))
        at(n, 10, (w_turn, 1))
        at(n, 11, (relay, 3))
        at(n, 12, (x_pass, 3))
        at(n, 14, (w_turn, 2))

        @pl.when(lax.rem(n, 8) == 0)
        def _():
            acc[...] = jnp.zeros_like(acc)

        head = pl.ds(pl.multiple_of((g * 4 + h) * DH, DH), DH)
        here = pl.ds(pl.multiple_of(t * T, T), T)
        q, do = q_s[here, head], do_s[here, head]
        top = jnp.full((8, T), -1e30, F32)
        for c in range(NK):
            s = dot(kv[g, rows(t, c), :], q, NT) + bias[t, c]
            s_ref[c] = s
            top = jnp.maximum(top, jnp.max(s.reshape(T // 8, 8, T), axis=0))
        top = jnp.max(top, axis=0, keepdims=True)
        weight = jnp.zeros((8, T), F32)
        for c in range(NK):
            e = jnp.exp2((s_ref[c] - top) * FACTOR2)
            s_ref[c] = e
            weight = weight + jnp.sum(e.reshape(T // 8, 8, T), axis=0)
        inverse = 1.0 / jnp.sum(weight, axis=0, keepdims=True)
        for c in range(NK):
            p = (s_ref[c] * inverse).astype(BF)
            p_ref[n, c] = p
            acc[rows(t, c), :] += dot(p, do, NN)

        @pl.when(lax.rem(n, 8) == 7)
        def _():
            gp[g] = acc[...].astype(BF)

        return 0

    lax.fori_loop(0, 16, phase1, 0)

    def dq_swap(g):
        block = pl.ds(g * 4 * DH, 4 * DH)
        place = cols(core * 2 + g, 4 * DH)
        return [
            remote(dq_s.at[rest, block], dq_out.at[:, place], psend.at[12 + g], precv.at[12 + g], partner),
            pltpu.make_async_copy(dq_s.at[half, block], dq_out.at[:, place], lsem.at[14 + g]),
        ]

    stays[6].wait()
    swaps[6].wait_recv()
    give_start(1)
    arrived(2)

    def phase2(n, _):
        g, h, t = n // 8, lax.rem(n // 2, 4), lax.rem(n, 2)
        at(n, 1, (give_sum, 0))
        at(n, 4, (w_turn, 3))
        at(n, 6, (give_total, 0))
        at(n, 7, (give_sum, 1))
        at(n, 8, (arrived, 3), (give_start, 2))
        at(n, 9, (x_pass, 1, 2))
        at(n, 12, (give_total, 1))
        at(n, 15, (w_part, 0), (give_sum, 2))

        @pl.when(lax.rem(n, 8) == 0)
        def _():
            acc[...] = jnp.zeros_like(acc)

        head = pl.ds(pl.multiple_of((g * 4 + h) * DH, DH), DH)
        here = pl.ds(pl.multiple_of(t * T, T), T)
        q, do = q_s[here, head], do_s[here, head]
        product = do.astype(F32) * o_s[here, head].astype(F32)
        delta = jnp.sum(jnp.transpose(product), axis=0, keepdims=True)
        for c in range(NK):
            dp = dot(kv[2 + g, rows(t, c), :], do, NT)
            ds = (p_ref[n, c].astype(F32) * (dp - delta)).astype(BF)
            p_ref[n, c] = ds
            acc[rows(t, c), :] += dot(ds, q, NN)

        @pl.when(lax.rem(n, 8) == 7)
        def _():
            gp[2 + g] = (acc[...] * FACTOR).astype(BF)

        return 0

    lax.fori_loop(0, 16, phase2, 0)
    give_start(3)
    w_across()

    def phase3(n, _):
        g, h, t = n // 8, lax.rem(n // 2, 4), lax.rem(n, 2)
        at(n, 3, (w_sum, 0), (w_part, 1))
        at(n, 8, (give_total, 2), (start_all, lambda: dq_swap(0)))
        at(n, 12, (w_sum, 1))
        at(n, 14, (give_sum, 3))
        dq = jnp.zeros((T, DH), F32)
        for c in range(NK):
            dq = dq + dot(p_ref[n, c], kv[g, rows(t, c), :], TN)
        head = pl.ds(pl.multiple_of((g * 4 + h) * DH, DH), DH)
        dq_s[pl.ds(pl.multiple_of(t * T, T), T), head] = (dq * FACTOR).astype(BF)
        return 0

    lax.fori_loop(0, 16, phase3, 0)
    for copy in dq_swap(1):
        copy.start()
    w_done()
    for i in range(8):
        a, j = i // 4, i % 4
        rows_of = weight[a, j].reshape(512, 4 * DH)
        in_out[:, i * 512 : (i + 1) * 512] = dot(vd[...], rows_of, NT).astype(BF)
    give_total(3)
    w_end(0)
    w_end(1)
    for g in (0, 1):
        for copy in dq_swap(g) + spread(2 + g) + keep(2 + g):
            copy.wait()
    for u in range(4):
        for k in (1, 2, 3):
            give(u, k).wait_send()

        @pl.when(has_prev)
        def _():
            back(u).wait_send()

    for copy in x_along():
        copy.wait_send()
    for i in range(7):
        swaps[i].wait_send()
    sg_swap.wait_send()
    for u in range(5):

        @pl.when(has_next)
        def _():
            forth(u).wait_send()

        for k in (1, 2, 3):
            along(u, k, 4).wait_send()


def attend(q, do, o, k, v, sg, x, w):
    dma = pltpu.SemaphoreType.DMA
    vmem = pltpu.VMEM
    return pl.pallas_call(
        main_kernel,
        in_specs=[ANY] * 5 + [VM, ANY, ANY],
        out_specs=[VM] * 4,
        out_shape=[
            jax.ShapeDtypeStruct((T, 16 * DH), BF),
            jax.ShapeDtypeStruct((T, 4 * DH), BF),
            jax.ShapeDtypeStruct((T, 4096), BF),
            jax.ShapeDtypeStruct((64, 4 * DH), F32),
        ],
        scratch_shapes=[
            vmem((CHIP, 8 * DH), BF),
            vmem((CHIP, 8 * DH), BF),
            vmem((CHIP, 8 * DH), BF),
            vmem((4, WIN, DH), BF),
            vmem((5, 2, 8, T), jnp.int32),
            vmem((2, NK, T, T), F32),
            vmem((NK, T, T), F32),
            vmem((16, NK, T, T), BF),
            vmem((WIN, DH), F32),
            vmem((CHIP, 8 * DH), BF),
            vmem((4, WIN, DH), BF),
            vmem((4, 3, CHIP, DH), BF),
            vmem((4, CHIP, DH), BF),
            vmem((4, CHIP, DH), BF),
            vmem((4, 2, T, DH), BF),
            vmem((T, 4 * DH), BF),
            vmem((2, 4, T, 2 * DH), BF),
            vmem((2, 4, 2, T, 512), BF),
            vmem((2, 2, 4, 128, DH), BF),
            vmem((2, 3, 2, 128, DH), BF),
            vmem((2, 2, 2, 64, DH), BF),
            vmem((2, 2, 8, 64, DH), BF),
            vmem((2, 4, 4, 2, 64, 4 * DH), BF),
            dma((20,)), dma((14,)), dma((14,)), dma((5,)), dma((5,)), dma((5, 3)), dma((5, 3)),
            dma((4, 3)), dma((4, 3)), dma((4,)), dma((4,)),
            dma((2, 3)), dma((2, 3)), dma((3, 2)), dma((3, 2)), dma((4,)), dma((4,)),
            dma((2, 3)), dma((2, 3)), dma((2, 2, 8)), dma((2, 2, 8)), dma((14,)), dma((14,)),
        ],
        compiler_params=pltpu.CompilerParams(
            collective_id=0, has_side_effects=True, vmem_limit_bytes=60 << 20
        ),
        name="attend",
    )(q, do, o, k, v, sg, x, w)


def on_device(
    inputs, value_weight, query_states, key_states, value_states, attention_out, out_grad, segment_ids
):
    query_grad, key_grad, input_grad, weight_grad = attend(
        query_states[0],
        out_grad[0],
        attention_out[0],
        key_states[0],
        value_states[0],
        segment_ids,
        inputs[0],
        value_weight,
    )
    return (query_grad[None], key_grad[None], input_grad[None], weight_grad)


def solution(mesh):
    placed = (
        P("dp", "ctx", None),
        P("ctx", None),
        P("dp", "ctx", None),
        P("dp", "ctx", None),
        P("dp", "ctx", None),
        P("dp", "ctx", None),
        P("dp", "ctx", None),
        P("dp", "ctx"),
    )
    return jax.shard_map(
        on_device,
        mesh=mesh,
        in_specs=placed,
        out_specs=(
            P("dp", "ctx", None),
            P("dp", "ctx", None),
            P("dp", "ctx", None),
            P("ctx", None),
        ),
        check_vma=False,
    )
```
